128 devices in a mesh: section: 8 (over y, core), table: 16 (over x, z).
Axes of the slice: x: 4, y: 4, z: 4, core: 2. Of those that a mesh axis runs over, the one named last changes fastest.
Arguments:
- emb_table: bfloat16 [524288, 128], P(('section', 'table')), may hold values from -6 to 6
- lcb_weight: bfloat16 [8, 512], replicated, may hold values from -0.25 to 0.25
- fm_proj: bfloat16 [8, 8, 128], P('section'), may hold values from -2 to 2
- norm_gain: bfloat16 [8, 1024], P('section'), may hold values from 0.25 to 1.75
- w_up: bfloat16 [8, 1024, 4096], P('section'), may hold values from -0.1875 to 0.1875
- w_down: bfloat16 [8, 4096, 1024], P('section'), may hold values from -0.09375 to 0.09375
- top_grad: bfloat16 [16, 4, 64, 1024], P('table'), may hold values from -12 to 12
- lookup_slot: int32 [16, 256, 512], P('table', 'section'), may hold values from 0 to 16383, as said below
- wanted_rows: int32 [128, 128, 128], P(('section', 'table')), may hold values from 0 to 4095, as said below
- row_counts: int32 [128, 128], P(('section', 'table')), may hold values from 32 to 128, as said below
Outputs:
- table_grad: float32 [524288, 128], P(('section', 'table'))
The draws below stay inside these ranges and needn't reach their ends.
Inputs may be any that keep to these rules, and one draw needn't show every extreme that they name: The first row_counts[o, q] entries of wanted_rows[o, q] are distinct rows; the others are also rows of the owner. `row_counts`: some owners have 128 live slots for every asking device. `lookup_slot`: A lookup of asking device q names slot o * 128 + c with c below row_counts[o, q].
All inputs are finite; a program needn't handle non-finite values.
Results may differ from the reference program's by a relative error of at most 0.025.
Values may be sent and summed in bfloat16 or wider, within the bound.
A program may use at most 128 MiB of HBM per device.

```python
import jax
import jax.numpy as jnp
from jax import lax

E = 128
K = 8
R = 128
D = 1024
H = 4096
F = 512
M = 4
B_DEV = 64
ROWS_DEV = 4096
CAP = 128
LAYERS = 8
SHARDS = 16
OWNERS = 128
LOOK_DEV = 32
N_SECTION = 8


def routing(key):
    base_key = jax.random.fold_in(key, 11)
    k_hot, k_load, k_jit, k_own, k_col = jax.random.split(base_key, 5)
    hot_count = max(1, OWNERS // 32)
    hot_ids = jax.random.permutation(k_hot, OWNERS)[:hot_count]
    is_hot = jnp.any(jnp.arange(OWNERS)[:, None] == hot_ids[None, :], axis=1)
    light_load = jax.random.randint(k_load, (OWNERS, OWNERS), max(1, CAP // 4), max(1, CAP // 2) + 1)
    counts = jnp.where(is_hot[:, None], CAP, light_load).astype(jnp.int32)
    stripe = ROWS_DEV // CAP
    jitter = jax.random.randint(k_jit, (OWNERS, OWNERS, CAP), 0, stripe)
    wanted = (jnp.arange(CAP)[None, None, :] * stripe + jitter).astype(jnp.int32)
    source = (jnp.arange(M * B_DEV) // LOOK_DEV)[None, :] * SHARDS + jnp.arange(SHARDS)[:, None]
    owner_ids = jax.random.randint(k_own, (SHARDS, M * B_DEV, F), 0, OWNERS)
    count_cap = counts[owner_ids, source[:, :, None]]
    column = jax.random.randint(k_col, (SHARDS, M * B_DEV, F), 0, 1 << 20) % count_cap
    slot_ids = (owner_ids * CAP + column).astype(jnp.int32)
    return (wanted, counts, slot_ids)


def draw_lookup_slot(key, part):
    return routing(key)[2]


def draw_wanted_rows(key, part):
    return routing(key)[0]


def draw_row_counts(key, part):
    return routing(key)[1]


def steps_of(own_key, extent, cuts, low, high):
    level, own = 1.0, jax.random.fold_in(own_key, 6)
    for axis_at, blocks in cuts:
        steps = jnp.exp(jax.random.uniform(jax.random.fold_in(own, axis_at), (blocks,), jnp.float32, low / len(cuts), high / len(cuts)))
        level = level * jnp.repeat(steps, extent[axis_at] // blocks).reshape([-1 if axis == axis_at else 1 for axis in range(len(extent))])
    return level


def bell_draw(stream_key, dims, spread, reach, cuts=(), kind=jnp.bfloat16):
    array = spread * jax.random.normal(stream_key, dims, jnp.float32)
    if cuts:
        array = array * steps_of(stream_key, dims, cuts, -0.22, 0.18)
    return jnp.clip(array, -reach, reach).astype(kind)


def setup_inputs(seed: int = 0) -> dict:
    streams_of = jax.random.split(jax.random.key(seed), 11)
    emb_table = bell_draw(streams_of[0], (OWNERS * ROWS_DEV, E), 1.0, 6.0, ((0, 128),))
    lcb_weight = bell_draw(streams_of[1], (K, F), F ** -0.5, 0.25)
    fm_proj = bell_draw(streams_of[2], (LAYERS, K, R), K ** -0.5, 2.0, ((0, 8),))
    norm_gain = jnp.clip(1.0 + 0.15 * jax.random.normal(streams_of[3], (LAYERS, D), jnp.float32), 0.25, 1.75).astype(jnp.bfloat16)
    w_up = bell_draw(streams_of[4], (LAYERS, D, H), D ** -0.5, 0.1875, ((0, 8),))
    w_down = bell_draw(streams_of[5], (LAYERS, H, D), H ** -0.5, 0.09375, ((0, 8),))
    top_grad = bell_draw(streams_of[6], (SHARDS, M, B_DEV, D), 2.0, 12.0, ((0, 16),))
    lookup_slot = draw_lookup_slot(jax.random.fold_in(streams_of[10], 71), 0)
    wanted_rows = draw_wanted_rows(jax.random.fold_in(streams_of[10], 71), 0)
    row_counts = draw_row_counts(jax.random.fold_in(streams_of[10], 71), 0)
    return {"emb_table": emb_table, "lcb_weight": lcb_weight, "fm_proj": fm_proj, "norm_gain": norm_gain, "w_up": w_up, "w_down": w_down, "top_grad": top_grad, "lookup_slot": lookup_slot, "wanted_rows": wanted_rows, "row_counts": row_counts}


EPSILON = 1e-05
DECAY_WEIGHT = 0.5

def fm_forward(inputs, proj, gain, w_up, w_down):
    batch_rows = inputs.shape[0]
    embed_count = proj.shape[0]
    features = inputs.reshape(batch_rows, embed_count, -1).astype(jnp.float32)
    mixed_cols = jnp.einsum('bke,kr->bre', features, proj.astype(jnp.float32)).astype(jnp.bfloat16)
    interact = jnp.einsum('bke,bre->bkr', features, mixed_cols.astype(jnp.float32)).reshape(batch_rows, -1)
    inv_scale = lax.rsqrt(lax.optimization_barrier(jnp.mean(interact * interact, axis=1, keepdims=True)) + EPSILON)
    normed = (interact * inv_scale * gain.astype(jnp.float32)).astype(jnp.bfloat16)
    before = jnp.dot(normed, w_up, preferred_element_type=jnp.float32)
    hidden = jnp.maximum(before, 0.0).astype(jnp.bfloat16)
    output = inputs.astype(jnp.float32) + jnp.dot(hidden, w_down, preferred_element_type=jnp.float32)
    return (output.astype(jnp.bfloat16), (features, mixed_cols, interact, inv_scale, before))

def fm_backward(inputs, grad_out, proj, gain, w_up, w_down):
    batch_rows = inputs.shape[0]
    embed_count = proj.shape[0]
    unused, saved = fm_forward(inputs, proj, gain, w_up, w_down)
    features, mixed_cols, interact, inv_scale, before = saved
    g_hidden = jnp.dot(grad_out, w_down.T, preferred_element_type=jnp.float32)
    g_before = jnp.where(before > 0.0, g_hidden, 0.0).astype(jnp.bfloat16)
    g_normed = jnp.dot(g_before, w_up.T, preferred_element_type=jnp.float32)
    weighted = g_normed * gain.astype(jnp.float32)
    g_interact = inv_scale * (weighted - interact * inv_scale * inv_scale * lax.optimization_barrier(jnp.mean(weighted * interact, axis=1, keepdims=True)))
    g_interact = g_interact.astype(jnp.bfloat16).reshape(batch_rows, embed_count, -1).astype(jnp.float32)
    g_features = jnp.einsum('bkr,bre->bke', g_interact, mixed_cols.astype(jnp.float32))
    g_mixed = jnp.einsum('bkr,bke->bre', g_interact, features).astype(jnp.bfloat16)
    g_features = g_features + jnp.einsum('bre,kr->bke', g_mixed.astype(jnp.float32), proj.astype(jnp.float32))
    return (grad_out.astype(jnp.float32) + g_features.reshape(batch_rows, -1)).astype(jnp.bfloat16)

def reference(emb_table, lcb_weight, fm_proj, norm_gain, w_up, w_down, top_grad, lookup_slot, wanted_rows, row_counts):
    look_dev = M * B_DEV // N_SECTION
    row_section = jnp.arange(M * B_DEV) // look_dev
    lcb_float = lcb_weight.astype(jnp.float32)

    def chain(pair):
        activ, grad_now = pair
        stash = []
        for layer in range(LAYERS):
            stash.append(activ)
            activ = fm_forward(activ, fm_proj[layer], norm_gain[layer], w_up[layer], w_down[layer])[0]
        for layer in reversed(range(LAYERS)):
            grad_now = fm_backward(stash[layer], grad_now, fm_proj[layer], norm_gain[layer], w_up[layer], w_down[layer])
        return grad_now

    def per_group(grads, group):
        source = row_section * SHARDS + group
        slots_here = lax.dynamic_index_in_dim(lookup_slot, group, 0, keepdims=False)
        owner_ids = slots_here // CAP
        column = slots_here % CAP
        row_id = owner_ids * ROWS_DEV + wanted_rows[owner_ids, source[:, None], column]
        embedded = emb_table[row_id].astype(jnp.float32)
        lead = jnp.einsum('kf,bfe->bke', lcb_float, embedded).astype(jnp.bfloat16).reshape(M, B_DEV, D)
        grads_top = lax.dynamic_index_in_dim(top_grad, group, 0, keepdims=False)
        lead_grad = lax.map(chain, (lead, grads_top))
        lead_grad = lead_grad.reshape(M * B_DEV, K, E).astype(jnp.float32)
        feature_grad = jnp.einsum('kf,bke->bfe', lcb_float, lead_grad)
        grads = grads.at[row_id.reshape(-1)].add(feature_grad.reshape(-1, E))
        return (grads, None)
    grads = jnp.zeros((OWNERS * ROWS_DEV, E), jnp.float32)
    grads, unused = lax.scan(per_group, grads, jnp.arange(SHARDS))

    def per_owner(grads, owner):
        local_rows = lax.dynamic_index_in_dim(wanted_rows, owner, 0, keepdims=False)
        counts_here = lax.dynamic_index_in_dim(row_counts, owner, 0, keepdims=False)
        live_slots = jnp.arange(CAP)[None, :] < counts_here[:, None]
        row_id = owner * ROWS_DEV + local_rows
        decay_term = jnp.where(live_slots[..., None], DECAY_WEIGHT * emb_table[row_id].astype(jnp.float32), 0.0)
        grads = grads.at[row_id.reshape(-1)].add(decay_term.reshape(-1, E))
        return (grads, None)
    grads, unused = lax.scan(per_owner, grads, jnp.arange(OWNERS))
    return grads
```

```python
import jax
import jax.numpy as jnp
from jax import lax
from jax.experimental import pallas as pl
from jax.experimental.pallas import tpu as pltpu
from jax.sharding import PartitionSpec as P

BF = jnp.bfloat16
F32 = jnp.float32
NT = (((1,), (1,)), ((), ()))
TN = (((0,), (0,)), ((), ()))


def gather_rows(table, ids):
    rows, width = table.shape
    count = ids.shape[0]
    block = 1024
    chunk = 128

    def body(idx, tab, out, wide, tmp):
        step = pl.program_id(0)

        @pl.when(step == 0)
        def _():
            wide[...] = tab[...].astype(F32)

        @pl.loop(0, block // chunk)
        def _(part):
            base = step * block + part * chunk
            for j in range(chunk):
                tmp[pl.ds(j, 1), :] = wide[pl.ds(idx[base + j], 1), :]
            out[pl.ds(pl.multiple_of(part * chunk, chunk), chunk), :] = tmp[...].astype(BF)

    return pl.pallas_call(
        body,
        grid=(count // block,),
        in_specs=[
            pl.BlockSpec(memory_space=pltpu.SMEM),
            pl.BlockSpec((rows, width), lambda i: (0, 0)),
        ],
        out_specs=pl.BlockSpec((block, width), lambda i: (i, 0)),
        out_shape=jax.ShapeDtypeStruct((count, width), BF),
        scratch_shapes=[pltpu.VMEM((rows, width), F32), pltpu.VMEM((chunk, width), F32)],
        name="gather_rows",
    )(ids, table)


def scatter_rows(values, ids, rows):
    count, width = values.shape
    block = 1024
    group = 16

    def body(idx, val, out, acc, wide, sem):
        step = pl.program_id(0)

        @pl.when(step == 0)
        def _():
            acc[...] = jnp.zeros_like(acc)

        wide[...] = val[...].astype(F32)

        @pl.loop(0, block // (4 * group))
        def _(part):
            for sub in range(4):
                at = part * (4 * group) + sub * group
                base = step * block + at
                where = [idx[base + j] for j in range(group)]
                new = [
                    acc[pl.ds(where[j], 1), :] + wide[pl.ds(at + j, 1), :]
                    for j in range(group)
                ]
                for j in range(group):
                    acc[pl.ds(where[j], 1), :] = new[j]

        @pl.when(step == pl.num_programs(0) - 1)
        def _():
            copy = pltpu.make_async_copy(acc.at[pl.ds(0, rows), :], out, sem)
            copy.start()
            copy.wait()

    return pl.pallas_call(
        body,
        grid=(count // block,),
        in_specs=[
            pl.BlockSpec(memory_space=pltpu.SMEM),
            pl.BlockSpec((block, width), lambda i: (i, 0)),
        ],
        out_specs=pl.BlockSpec(memory_space=pl.ANY),
        out_shape=jax.ShapeDtypeStruct((rows, width), F32),
        scratch_shapes=[
            pltpu.VMEM((rows + 8, width), F32),
            pltpu.VMEM((block, width), F32),
            pltpu.SemaphoreType.DMA,
        ],
        name="scatter_rows",
    )(ids, values)


def lookup_matrix(slots, lcb, owners, cap):
    samples, features = slots.shape
    embeds = lcb.shape[0]
    shift = cap.bit_length() - 1

    def body(slot_ref, lcb_ref, out_ref):
        tiled = jnp.concatenate([lcb_ref[...].astype(F32)] * 2, axis=0).astype(BF)
        zero = jnp.zeros((), BF)
        lane_c = lax.broadcasted_iota(jnp.int32, (cap, features), 0)
        parts = []
        for h in range(2):
            slot = slot_ref[0, pl.ds(h, 1), :]
            owner = lax.shift_right_logical(slot, shift)
            col = slot & (cap - 1)
            picks = jnp.where(lane_c == col, 1.0, 0.0).astype(BF)
            owner16 = jnp.broadcast_to(owner.astype(F32), (16, features)).astype(BF)
            row = (lax.broadcasted_iota(jnp.int32, (16, features), 0) // embeds).astype(F32).astype(BF)
            rows = []
            for o in range(0, owners, 2):
                rows.append(jnp.where(owner16 == row + jnp.asarray(float(o), BF), tiled, zero))
            spread = jnp.concatenate(rows, axis=0)
            got = lax.dot_general(spread, picks, NT, preferred_element_type=F32)
            parts.append(got.reshape(owners // 2, 2, embeds, cap))
        for par in range(2):
            both = jnp.concatenate([parts[0][:, par], parts[1][:, par]], axis=1)
            out_ref[:, :, par * cap : (par + 1) * cap] = both.astype(BF)

    return pl.pallas_call(
        body,
        grid=(samples // 2,),
        in_specs=[
            pl.BlockSpec((1, 2, features), lambda i: (i, 0, 0)),
            pl.BlockSpec((embeds, features), lambda i: (0, 0)),
        ],
        out_specs=pl.BlockSpec((owners // 2, 2 * embeds, 2 * cap), lambda i: (0, i, 0)),
        out_shape=jax.ShapeDtypeStruct((owners // 2, samples * embeds, 2 * cap), BF),
        cost_estimate=pl.CostEstimate(flops=2 * samples * owners * embeds * cap * features, bytes_accessed=16 << 20, transcendentals=0),
        name="lookup_matrix",
    )(slots.reshape(samples // 2, 2, features), lcb)


def compress(matrix, fetched):
    pairs, outs, slots = matrix.shape
    width = fetched.shape[1]
    step_pairs = 8

    def body(mat, rows, out, acc):
        step = pl.program_id(0)

        @pl.when(step == 0)
        def _():
            acc[...] = jnp.zeros_like(acc)

        total = acc[...]
        for i in range(step_pairs):
            total += jnp.dot(mat[i], rows[pl.ds(i * slots, slots), :], preferred_element_type=F32)
        acc[...] = total

        @pl.when(step == pl.num_programs(0) - 1)
        def _():
            out[...] = acc[...].astype(BF)

    return pl.pallas_call(
        body,
        grid=(pairs // step_pairs,),
        in_specs=[
            pl.BlockSpec((step_pairs, outs, slots), lambda i: (i, 0, 0)),
            pl.BlockSpec((step_pairs * slots, width), lambda i: (i, 0)),
        ],
        out_specs=pl.BlockSpec((outs, width), lambda i: (0, 0)),
        out_shape=jax.ShapeDtypeStruct((outs, width), BF),
        scratch_shapes=[pltpu.VMEM((outs, width), F32)],
        name="compress",
    )(matrix, fetched)


def expand(matrix, grads, fetched, decay):
    pairs, outs, slots = matrix.shape
    width = fetched.shape[1]
    step_pairs = 8

    def body(mat, grad, rows, out):
        for i in range(step_pairs):
            at = pl.ds(i * slots, slots)
            got = lax.dot_general(mat[i], grad[...], TN, preferred_element_type=F32)
            out[at, :] = (got + decay * rows[at, :].astype(F32)).astype(BF)

    return pl.pallas_call(
        body,
        grid=(pairs // step_pairs,),
        in_specs=[
            pl.BlockSpec((step_pairs, outs, slots), lambda i: (i, 0, 0)),
            pl.BlockSpec((outs, width), lambda i: (0, 0)),
            pl.BlockSpec((step_pairs * slots, width), lambda i: (i, 0)),
        ],
        out_specs=pl.BlockSpec((step_pairs * slots, width), lambda i: (i, 0)),
        out_shape=jax.ShapeDtypeStruct((pairs * slots, width), BF),
        name="expand",
    )(matrix, grads, fetched)


EPSILON = 1e-05
DECAY_WEIGHT = 0.5


def shifted(value, axis, steps):
    count = lax.axis_size(axis)
    first, last = (max(0, -steps), min(count, count - steps))
    return lax.ppermute(value, axis, [(source, source + steps) for source in range(first, last)])


def broadcast(block, axis, holder):
    block = jnp.where(lax.axis_index(axis) == holder, block, jnp.zeros_like(block))
    return lax.psum(block, axis)


def fm_forward(inputs, proj, gain, w_up, w_down):
    batch_rows = inputs.shape[0]
    embed_count = proj.shape[0]
    features = inputs.reshape(batch_rows, embed_count, -1)
    mixed_cols = jnp.einsum(
        "bke,kr->bre", features, proj, preferred_element_type=jnp.float32
    ).astype(jnp.bfloat16)
    interact = jnp.einsum(
        "bke,bre->bkr", features, mixed_cols, preferred_element_type=jnp.float32
    ).reshape(batch_rows, -1)
    inv_scale = lax.rsqrt(jnp.mean(interact * interact, axis=1, keepdims=True) + EPSILON)
    normed = (interact * inv_scale * gain.astype(jnp.float32)).astype(jnp.bfloat16)
    before = jnp.dot(normed, w_up, preferred_element_type=jnp.float32)
    hidden = jnp.maximum(before, 0.0).astype(jnp.bfloat16)
    output = inputs.astype(jnp.float32) + jnp.dot(
        hidden, w_down, preferred_element_type=jnp.float32
    )
    return (output.astype(jnp.bfloat16), (features, mixed_cols, interact, inv_scale, before))


def fm_backward(inputs, grad_out, proj, gain, w_up, w_down):
    batch_rows = inputs.shape[0]
    embed_count = proj.shape[0]
    unused, saved = fm_forward(inputs, proj, gain, w_up, w_down)
    features, mixed_cols, interact, inv_scale, before = saved
    last_dims = (((1,), (1,)), ((), ()))
    g_hidden = lax.dot_general(grad_out, w_down, last_dims, preferred_element_type=jnp.float32)
    g_before = jnp.where(before > 0.0, g_hidden, 0.0).astype(jnp.bfloat16)
    g_normed = lax.dot_general(g_before, w_up, last_dims, preferred_element_type=jnp.float32)
    weighted = g_normed * gain.astype(jnp.float32)
    g_interact = inv_scale * (
        weighted
        - interact * inv_scale * inv_scale * jnp.mean(weighted * interact, axis=1, keepdims=True)
    )
    g_interact = g_interact.astype(jnp.bfloat16).reshape(batch_rows, embed_count, -1)
    g_features = jnp.einsum(
        "bkr,bre->bke", g_interact, mixed_cols, preferred_element_type=jnp.float32
    )
    g_mixed = jnp.einsum(
        "bkr,bke->bre", g_interact, features, preferred_element_type=jnp.float32
    ).astype(jnp.bfloat16)
    g_features = g_features + jnp.einsum(
        "bre,kr->bke", g_mixed, proj, preferred_element_type=jnp.float32
    )
    return (grad_out.astype(jnp.float32) + g_features.reshape(batch_rows, -1)).astype(jnp.bfloat16)


def pass_on(payload, offset):
    return shifted(payload, "section", offset)


def per_device(
    emb_table,
    lcb_weight,
    fm_proj,
    norm_gain,
    w_up,
    w_down,
    top_grad,
    lookup_slot,
    wanted_rows,
    row_counts,
):
    section_count = lax.axis_size("section")
    shard_count = lax.axis_size("table")
    my_section = lax.axis_index("section")
    owners = section_count * shard_count
    cap = wanted_rows.shape[2]
    embed_width = emb_table.shape[1]
    picked_rows = wanted_rows[0]
    outgoing = gather_rows(emb_table, picked_rows.reshape(-1)).reshape(owners, cap, embed_width)
    fetched = lax.all_to_all(
        outgoing, ("section", "table"), split_axis=0, concat_axis=0, tiled=True
    )
    fetched = fetched.reshape(owners * cap, embed_width)
    lookup_slots = lookup_slot[0]
    look_dev = lookup_slots.shape[0]
    matrix = lookup_matrix(lookup_slots, lcb_weight, owners, cap)
    compressed = compress(matrix, fetched).reshape(look_dev, -1)
    leading = lax.all_gather(compressed, "section", axis=0, tiled=True)
    micro_count = top_grad.shape[1]
    batch_rows = top_grad.shape[2]
    model_width = top_grad.shape[3]
    leading = leading.reshape(micro_count, batch_rows, model_width)
    weights = (fm_proj[0], norm_gain[0], w_up[0], w_down[0])
    tick_count = micro_count + section_count - 1

    def forward_tick(tick, state):
        incoming, stash = state
        micro_idx = tick - my_section
        is_valid = (micro_idx >= 0) & (micro_idx < micro_count)
        clipped = jnp.clip(micro_idx, 0, micro_count - 1)
        inputs = jnp.where(
            my_section == 0, lax.dynamic_index_in_dim(leading, clipped, 0, keepdims=False), incoming
        )
        outputs = lax.cond(
            is_valid,
            lambda value: fm_forward(value, *weights)[0],
            lambda value: jnp.zeros_like(value),
            inputs,
        )
        kept_rows = jnp.where(
            is_valid, inputs, lax.dynamic_index_in_dim(stash, clipped, 0, keepdims=False)
        )
        stash = lax.dynamic_update_index_in_dim(stash, kept_rows, clipped, 0)
        return (pass_on(outputs, 1), stash)

    empty_rows = jnp.zeros((batch_rows, model_width), jnp.bfloat16)
    empty_stash = jnp.zeros((micro_count, batch_rows, model_width), jnp.bfloat16)
    unused, stash = lax.fori_loop(0, tick_count, forward_tick, (empty_rows, empty_stash))
    grads_top = top_grad[0]

    def backward_tick(tick, state):
        incoming, lead_grad = state
        micro_idx = tick - (section_count - 1 - my_section)
        is_valid = (micro_idx >= 0) & (micro_idx < micro_count)
        clipped = jnp.clip(micro_idx, 0, micro_count - 1)
        given = jnp.where(
            my_section == section_count - 1,
            lax.dynamic_index_in_dim(grads_top, clipped, 0, keepdims=False),
            incoming,
        )
        saved_rows = lax.dynamic_index_in_dim(stash, clipped, 0, keepdims=False)
        result = lax.cond(
            is_valid,
            lambda pair: fm_backward(pair[0], pair[1], *weights),
            lambda pair: jnp.zeros_like(pair[0]),
            (saved_rows, given),
        )
        record = jnp.where(
            is_valid & (my_section == 0),
            result,
            lax.dynamic_index_in_dim(lead_grad, clipped, 0, keepdims=False),
        )
        lead_grad = lax.dynamic_update_index_in_dim(lead_grad, record, clipped, 0)
        return (pass_on(result, -1), lead_grad)

    unused, lead_grad = lax.fori_loop(0, tick_count, backward_tick, (empty_rows, empty_stash))
    whole_grad = broadcast(lead_grad, "section", 0).reshape(micro_count * batch_rows, model_width)
    lead_share = lax.dynamic_slice_in_dim(whole_grad, my_section * look_dev, look_dev, 0)
    slot_grad = expand(matrix, lead_share.reshape(-1, embed_width), fetched, DECAY_WEIGHT)
    returned = lax.all_to_all(
        slot_grad.reshape(owners, cap, embed_width),
        ("section", "table"),
        split_axis=0,
        concat_axis=0,
        tiled=True,
    ).reshape(owners * cap, embed_width)
    rows_here = emb_table.shape[0]
    live_slots = jnp.arange(cap)[None, :] < row_counts[0][:, None]
    targets = jnp.where(live_slots, picked_rows, rows_here).reshape(-1)
    return scatter_rows(returned, targets, rows_here)


def solution(mesh):
    in_specs = (
        P(("section", "table"), None),
        P(),
        P("section", None, None),
        P("section", None),
        P("section", None, None),
        P("section", None, None),
        P("table", None, None, None),
        P("table", "section", None),
        P(("section", "table"), None, None),
        P(("section", "table"), None),
    )
    out_specs = P(("section", "table"), None)
    return jax.shard_map(
        per_device, mesh=mesh, in_specs=in_specs, out_specs=out_specs, check_vma=False
    )
```

```python
import jax
import jax.numpy as jnp
from jax import lax
from jax.experimental import pallas as pl
from jax.experimental.pallas import tpu as pltpu
from jax.sharding import PartitionSpec as P

BF = jnp.bfloat16
F32 = jnp.float32
NT = (((1,), (1,)), ((), ()))
TN = (((0,), (0,)), ((), ()))
EPSILON = 1e-05
DECAY_WEIGHT = 0.5
MICRO_ROWS = 64


def gather_rows(table, ids):
    rows, width = table.shape
    count = ids.shape[0]
    block = 1024
    chunk = 128

    def body(idx, tab, out, wide, tmp):
        step = pl.program_id(0)

        @pl.when(step == 0)
        def _():
            wide[...] = tab[...].astype(F32)

        @pl.loop(0, block // chunk)
        def _(part):
            base = step * block + part * chunk
            for j in range(chunk):
                tmp[pl.ds(j, 1), :] = wide[pl.ds(idx[base + j], 1), :]
            out[pl.ds(pl.multiple_of(part * chunk, chunk), chunk), :] = tmp[...].astype(BF)

    return pl.pallas_call(
        body,
        grid=(count // block,),
        in_specs=[
            pl.BlockSpec(memory_space=pltpu.SMEM),
            pl.BlockSpec((rows, width), lambda i: (0, 0)),
        ],
        out_specs=pl.BlockSpec((block, width), lambda i: (i, 0)),
        out_shape=jax.ShapeDtypeStruct((count, width), BF),
        scratch_shapes=[pltpu.VMEM((rows, width), F32), pltpu.VMEM((chunk, width), F32)],
        name="gather_rows",
    )(ids, table)


def scatter_rows(values, ids, rows):
    count, width = values.shape
    block = 1024
    group = 16

    def body(idx, val, out, acc, wide, sem):
        step = pl.program_id(0)

        @pl.when(step == 0)
        def _():
            acc[...] = jnp.zeros_like(acc)

        wide[...] = val[...].astype(F32)

        @pl.loop(0, block // (4 * group))
        def _(part):
            for sub in range(4):
                at = part * (4 * group) + sub * group
                base = step * block + at
                where = [idx[base + j] for j in range(group)]
                new = [
                    acc[pl.ds(where[j], 1), :] + wide[pl.ds(at + j, 1), :]
                    for j in range(group)
                ]
                for j in range(group):
                    acc[pl.ds(where[j], 1), :] = new[j]

        @pl.when(step == pl.num_programs(0) - 1)
        def _():
            copy = pltpu.make_async_copy(acc.at[pl.ds(0, rows), :], out, sem)
            copy.start()
            copy.wait()

    return pl.pallas_call(
        body,
        grid=(count // block,),
        in_specs=[
            pl.BlockSpec(memory_space=pltpu.SMEM),
            pl.BlockSpec((block, width), lambda i: (i, 0)),
        ],
        out_specs=pl.BlockSpec(memory_space=pl.ANY),
        out_shape=jax.ShapeDtypeStruct((rows, width), F32),
        scratch_shapes=[
            pltpu.VMEM((rows + 8, width), F32),
            pltpu.VMEM((block, width), F32),
            pltpu.SemaphoreType.DMA,
        ],
        name="scatter_rows",
    )(ids, values)


def lookup_matrix(slots, lcb, owners, cap):
    samples, features = slots.shape
    embeds = lcb.shape[0]
    shift = cap.bit_length() - 1

    def body(slot_ref, lcb_ref, out_ref):
        tiled = jnp.concatenate([lcb_ref[...].astype(F32)] * 2, axis=0).astype(BF)
        zero = jnp.zeros((), BF)
        lane_c = lax.broadcasted_iota(jnp.int32, (cap, features), 0)
        parts = []
        for h in range(2):
            slot = slot_ref[0, pl.ds(h, 1), :]
            owner = lax.shift_right_logical(slot, shift)
            col = slot & (cap - 1)
            picks = jnp.where(lane_c == col, 1.0, 0.0).astype(BF)
            owner16 = jnp.broadcast_to(owner.astype(F32), (16, features)).astype(BF)
            row = (lax.broadcasted_iota(jnp.int32, (16, features), 0) // embeds).astype(F32).astype(BF)
            rows = []
            for o in range(0, owners, 2):
                rows.append(jnp.where(owner16 == row + jnp.asarray(float(o), BF), tiled, zero))
            spread = jnp.concatenate(rows, axis=0)
            got = lax.dot_general(spread, picks, NT, preferred_element_type=F32)
            parts.append(got.reshape(owners // 2, 2, embeds, cap))
        for par in range(2):
            both = jnp.concatenate([parts[0][:, par], parts[1][:, par]], axis=1)
            out_ref[:, :, par * cap : (par + 1) * cap] = both.astype(BF)

    return pl.pallas_call(
        body,
        grid=(samples // 2,),
        in_specs=[
            pl.BlockSpec((1, 2, features), lambda i: (i, 0, 0)),
            pl.BlockSpec((embeds, features), lambda i: (0, 0)),
        ],
        out_specs=pl.BlockSpec((owners // 2, 2 * embeds, 2 * cap), lambda i: (0, i, 0)),
        out_shape=jax.ShapeDtypeStruct((owners // 2, samples * embeds, 2 * cap), BF),
        cost_estimate=pl.CostEstimate(flops=2 * samples * owners * embeds * cap * features, bytes_accessed=16 << 20, transcendentals=0),
        name="lookup_matrix",
    )(slots.reshape(samples // 2, 2, features), lcb)


def compress(matrix, fetched):
    pairs, outs, slots = matrix.shape
    width = fetched.shape[1]
    step_pairs = 8

    def body(mat, rows, out, acc):
        step = pl.program_id(0)

        @pl.when(step == 0)
        def _():
            acc[...] = jnp.zeros_like(acc)

        total = acc[...]
        for i in range(step_pairs):
            total += jnp.dot(mat[i], rows[pl.ds(i * slots, slots), :], preferred_element_type=F32)
        acc[...] = total

        @pl.when(step == pl.num_programs(0) - 1)
        def _():
            out[...] = acc[...].astype(BF)

    return pl.pallas_call(
        body,
        grid=(pairs // step_pairs,),
        in_specs=[
            pl.BlockSpec((step_pairs, outs, slots), lambda i: (i, 0, 0)),
            pl.BlockSpec((step_pairs * slots, width), lambda i: (i, 0)),
        ],
        out_specs=pl.BlockSpec((outs, width), lambda i: (0, 0)),
        out_shape=jax.ShapeDtypeStruct((outs, width), BF),
        scratch_shapes=[pltpu.VMEM((outs, width), F32)],
        name="compress",
    )(matrix, fetched)


def expand(matrix, grads, fetched, decay):
    pairs, outs, slots = matrix.shape
    width = fetched.shape[1]
    step_pairs = 8

    def body(mat, grad, rows, out):
        for i in range(step_pairs):
            at = pl.ds(i * slots, slots)
            got = lax.dot_general(mat[i], grad[...], TN, preferred_element_type=F32)
            out[at, :] = (got + decay * rows[at, :].astype(F32)).astype(BF)

    return pl.pallas_call(
        body,
        grid=(pairs // step_pairs,),
        in_specs=[
            pl.BlockSpec((step_pairs, outs, slots), lambda i: (i, 0, 0)),
            pl.BlockSpec((outs, width), lambda i: (0, 0)),
            pl.BlockSpec((step_pairs * slots, width), lambda i: (i, 0)),
        ],
        out_specs=pl.BlockSpec((step_pairs * slots, width), lambda i: (i, 0)),
        out_shape=jax.ShapeDtypeStruct((pairs * slots, width), BF),
        name="expand",
    )(matrix, grads, fetched)


def layer_forward(a_ref, proj, gain, w_up, w_down, keep, out_ref, last):
    interact, inv_keep, hidden, wide, unit = keep
    rows = a_ref.shape[0]
    embeds, width = proj.shape
    model = gain.shape[1]
    inner = w_up.shape[1]
    wide[...] = a_ref[...].astype(F32)

    def block(i, carry):
        at = pl.ds(pl.multiple_of(i * 8, 8), 8)
        p = [jnp.broadcast_to(proj[k : k + 1, :], (8, width)) for k in range(embeds)]
        a = [wide[at, k * width : (k + 1) * width] for k in range(embeds)]
        gram = {}
        for k in range(embeds):
            for q in range(k, embeds):
                gram[k, q] = gram[q, k] = jnp.sum(a[k] * a[q], axis=1, keepdims=True)
        square = None
        mixed = []
        for k in range(embeds):
            total = gram[k, 0] * p[0]
            for q in range(1, embeds):
                total += gram[k, q] * p[q]
            mixed.append(total)
            interact[at, k * width : (k + 1) * width] = total
            square = total * total if square is None else square + total * total
        inv = lax.rsqrt(jnp.sum(square, axis=1, keepdims=True) * (1.0 / model) + EPSILON)
        inv_keep[at, :] = jnp.broadcast_to(inv, (8, width))
        for k in range(embeds):
            cols = slice(k * width, (k + 1) * width)
            unit[at, cols] = mixed[k] * inv * gain[:, cols]
        return carry

    lax.fori_loop(0, rows // 8, block, 0, unroll=2)
    normed = unit[...].astype(BF)
    tile = min(512, inner)
    for n in range(0, inner, tile):
        before = jnp.dot(normed, w_up[:, n : n + tile], preferred_element_type=F32)
        hidden[:, n : n + tile] = jnp.maximum(before, 0.0).astype(BF)

    @pl.when(jnp.logical_not(last))
    def _():
        tile = 256
        for n in range(0, model, tile):
            got = jnp.dot(hidden[...], w_down[:, n : n + tile], preferred_element_type=F32)
            out_ref[:, n : n + tile] = (got + a_ref[:, n : n + tile].astype(F32)).astype(BF)


def layer_backward(a_ref, g_ref, proj, gain, up_t, down_t, keep, gated, out_ref):
    interact, inv_keep, hidden, wide, unit = keep
    rows = a_ref.shape[0]
    embeds, width = proj.shape
    model = gain.shape[1]
    inner = down_t.shape[1]
    g = g_ref[...]
    tile = min(512, inner)
    for n in range(0, inner, tile):
        up = jnp.dot(g, down_t[:, n : n + tile], preferred_element_type=F32)
        gated[:, n : n + tile] = jnp.where(hidden[:, n : n + tile].astype(F32) > 0.0, up, 0.0).astype(BF)
    tile = 256
    for n in range(0, model, tile):
        unit[:, n : n + tile] = jnp.dot(gated[...], up_t[:, n : n + tile], preferred_element_type=F32)
    wide[...] = a_ref[...].astype(F32)

    def block(i, carry):
        at = pl.ds(pl.multiple_of(i * 8, 8), 8)
        cols = [slice(k * width, (k + 1) * width) for k in range(embeds)]
        weighted = [unit[at, cols[k]] * gain[:, cols[k]] for k in range(embeds)]
        mixed = [interact[at, cols[k]] for k in range(embeds)]
        cross = weighted[0] * mixed[0]
        for k in range(1, embeds):
            cross += weighted[k] * mixed[k]
        mean = jnp.sum(cross, axis=1, keepdims=True) * (1.0 / model)
        inv = inv_keep[at, :]
        slope = inv * inv * mean
        grad = [inv * (weighted[k] - mixed[k] * slope) for k in range(embeds)]
        p = [jnp.broadcast_to(proj[k : k + 1, :], (8, width)) for k in range(embeds)]
        pair = {}
        for k in range(embeds):
            for q in range(k, embeds):
                term = grad[k] * p[q] + grad[q] * p[k]
                pair[k, q] = pair[q, k] = jnp.sum(term, axis=1, keepdims=True)
        a = [wide[at, cols[k]] for k in range(embeds)]
        for k in range(embeds):
            total = pair[k, 0] * a[0]
            for q in range(1, embeds):
                total += pair[k, q] * a[q]
            unit[at, cols[k]] = total
        return carry

    lax.fori_loop(0, rows // 8, block, 0, unroll=2)
    out_ref[...] = (unit[...] + g_ref[...].astype(F32)).astype(BF)


def layer_pipeline(shares, top, proj, gain, w_up, w_down, up_t, down_t, stages, rows):
    look, model = shares.shape
    micro = top.shape[0] // rows
    per = rows // look
    inner = w_up.shape[1]
    width = proj.shape[1]
    copy_to = pltpu.make_async_remote_copy
    copy_here = pltpu.make_async_copy

    def body(
        share_in, top_in, proj_ref, gain_ref, up_in, down_in, up_t_in, down_t_in, out,
        acts, cots, acts_out, cots_out, share, up_v, down_v, up_tv, down_tv,
        interact, inv_keep, hidden, wide, unit, gated,
        wsem, tsem, fsend, frecv, gsend, grecv, isend, irecv, osend, orecv, lsem,
    ):
        me = lax.axis_index("section")
        first, last = me == 0, me == stages - 1
        loads = [
            copy_here(src, dst, wsem.at[i])
            for i, (src, dst) in enumerate(
                [(up_in, up_v), (down_in, down_v), (down_t_in, down_tv), (up_t_in, up_tv)]
            )
        ]
        loads[0].start()
        loads[1].start()
        tops = [copy_here(top_in.at[pl.ds(m * rows, rows), :], cots.at[m], tsem.at[m]) for m in range(micro)]

        @pl.when(last)
        def _():
            for m in range(micro):
                tops[m].start()

        barrier = pltpu.get_barrier_semaphore()
        for d in range(1, stages):
            pl.semaphore_signal(
                barrier, inc=1, device_id={"section": lax.rem(me + d, stages)},
                device_id_type=pl.DeviceIdType.MESH,
            )
        pl.semaphore_wait(barrier, stages - 1)

        def entry(section):
            slot, off = section // per, lax.rem(section, per) * look
            return copy_to(
                src_ref=share_in, dst_ref=acts.at[slot, pl.ds(pl.multiple_of(off, look), look), :],
                send_sem=isend, recv_sem=irecv.at[section],
                device_id={"section": 0}, device_id_type=pl.DeviceIdType.MESH,
            )

        own = copy_here(share_in, acts.at[0, pl.ds(0, look), :], irecv.at[0])

        @pl.when(first)
        def _():
            own.start()
            own.wait()
            for section in range(1, stages):
                entry(jnp.int32(section)).wait_recv()

        @pl.when(jnp.logical_not(first))
        def _():
            entry(me).start()

        def onward(m):
            return copy_to(
                src_ref=acts_out.at[m], dst_ref=acts.at[m], send_sem=fsend.at[m], recv_sem=frecv.at[m],
                device_id={"section": lax.rem(me + 1, stages)}, device_id_type=pl.DeviceIdType.MESH,
            )

        def back(m):
            return copy_to(
                src_ref=cots_out.at[m], dst_ref=cots.at[m], send_sem=gsend.at[m], recv_sem=grecv.at[m],
                device_id={"section": lax.rem(me + stages - 1, stages)}, device_id_type=pl.DeviceIdType.MESH,
            )

        def leave(m, j, section):
            return copy_to(
                src_ref=cots_out.at[m, pl.ds(j * look, look), :], dst_ref=share,
                send_sem=osend.at[section], recv_sem=orecv,
                device_id={"section": section}, device_id_type=pl.DeviceIdType.MESH,
            )

        keep_own = copy_here(cots_out.at[0, pl.ds(0, look), :], share, lsem)
        loads[0].wait()
        loads[1].wait()
        loads[2].start()
        loads[3].start()

        def step(i, carry):
            ahead = jnp.where(last, lax.rem(i, 2) == 0, i < micro)
            m = jnp.where(last, i // 2, lax.rem(i, micro))
            keep = (interact.at[m], inv_keep.at[m], hidden.at[m], wide, unit)

            @pl.when(ahead)
            def _():
                @pl.when(jnp.logical_not(first))
                def _():
                    onward(m).wait_recv()

                layer_forward(acts.at[m], proj_ref, gain_ref, up_v, down_v, keep, acts_out.at[m], last)

                @pl.when(jnp.logical_not(last))
                def _():
                    onward(m).start()

            @pl.when(jnp.logical_not(ahead))
            def _():
                @pl.when(m == 0)
                def _():
                    loads[2].wait()
                    loads[3].wait()

                @pl.when(last)
                def _():
                    copy_here(top_in.at[pl.ds(pl.multiple_of(m * rows, rows), rows), :], cots.at[m], tsem.at[m]).wait()

                @pl.when(jnp.logical_not(last))
                def _():
                    back(m).wait_recv()

                layer_backward(
                    acts.at[m], cots.at[m], proj_ref, gain_ref, up_tv, down_tv, keep, gated, cots_out.at[m]
                )

                @pl.when(jnp.logical_not(first))
                def _():
                    back(m).start()

                @pl.when(first)
                def _():
                    for j in range(per):
                        section = m * per + j
                        if j == 0:
                            @pl.when(section == 0)
                            def _():
                                keep_own.start()

                            @pl.when(section > 0)
                            def _():
                                leave(m, j, section).start()
                        else:
                            leave(m, j, section).start()

            return carry

        lax.fori_loop(0, 2 * micro, step, 0)

        @pl.when(first)
        def _():
            keep_own.wait()
            for section in range(1, stages):
                leave(section // per, section % per, jnp.int32(section)).wait_send()

        @pl.when(jnp.logical_not(first))
        def _():
            leave(0, 0, jnp.int32(0)).wait_recv()
            entry(me).wait_send()
            for m in range(micro):
                back(m).wait_send()

        @pl.when(jnp.logical_not(last))
        def _():
            for m in range(micro):
                onward(m).wait_send()

        out[...] = share[...]

    vmem = pl.BlockSpec(memory_space=pltpu.VMEM)
    hbm = pl.BlockSpec(memory_space=pl.ANY)
    dma = pltpu.SemaphoreType.DMA
    block = (micro, rows, model)
    return pl.pallas_call(
        body,
        in_specs=[vmem, hbm, vmem, vmem, hbm, hbm, hbm, hbm],
        out_specs=vmem,
        out_shape=jax.ShapeDtypeStruct((look, model), BF),
        scratch_shapes=[
            pltpu.VMEM(block, BF), pltpu.VMEM(block, BF), pltpu.VMEM(block, BF), pltpu.VMEM(block, BF),
            pltpu.VMEM((look, model), BF),
            pltpu.VMEM((model, inner), BF), pltpu.VMEM((inner, model), BF),
            pltpu.VMEM((inner, model), BF), pltpu.VMEM((model, inner), BF),
            pltpu.VMEM(block, F32), pltpu.VMEM((micro, rows, width), F32), pltpu.VMEM((micro, rows, inner), BF),
            pltpu.VMEM((rows, model), F32), pltpu.VMEM((rows, model), F32), pltpu.VMEM((rows, inner), BF),
            dma((4,)), dma((micro,)), dma((micro,)), dma((micro,)), dma((micro,)), dma((micro,)),
            dma, dma((stages,)), dma((stages,)), dma, dma,
        ],
        compiler_params=pltpu.CompilerParams(
            collective_id=0, has_side_effects=True, vmem_limit_bytes=60 << 20
        ),
        name="layer_pipeline",
    )(shares, top, proj, gain, w_up, w_down, up_t, down_t)


def per_device(
    emb_table,
    lcb_weight,
    fm_proj,
    norm_gain,
    w_up,
    w_down,
    top_grad,
    lookup_slot,
    wanted_rows,
    row_counts,
):
    section_count = lax.axis_size("section")
    owners = section_count * lax.axis_size("table")
    cap = wanted_rows.shape[2]
    rows_here, embed_width = emb_table.shape
    picked_rows = wanted_rows[0]

    def exchange(rows):
        rows = rows.reshape(owners, cap, embed_width)
        rows = lax.all_to_all(rows, ("section", "table"), split_axis=0, concat_axis=0, tiled=True)
        return rows.reshape(owners * cap, embed_width)

    fetched = exchange(gather_rows(emb_table, picked_rows.reshape(-1)))
    lookup_slots = lookup_slot[0]
    look_dev = lookup_slots.shape[0]
    matrix = lookup_matrix(lookup_slots, lcb_weight, owners, cap)
    shares = compress(matrix, fetched).reshape(look_dev, -1)
    model_width = top_grad.shape[3]
    lead_share = layer_pipeline(
        shares,
        top_grad.reshape(-1, model_width),
        fm_proj[0].astype(F32),
        norm_gain.astype(F32),
        w_up[0],
        w_down[0],
        w_up[0].T,
        w_down[0].T,
        section_count,
        MICRO_ROWS,
    )
    slot_grad = expand(matrix, lead_share.reshape(-1, embed_width), fetched, DECAY_WEIGHT)
    returned = exchange(slot_grad)
    live_slots = jnp.arange(cap)[None, :] < row_counts[0][:, None]
    targets = jnp.where(live_slots, picked_rows, rows_here).reshape(-1)
    return scatter_rows(returned, targets, rows_here)


def solution(mesh):
    in_specs = (
        P(("section", "table"), None),
        P(),
        P("section", None, None),
        P("section", None),
        P("section", None, None),
        P("section", None, None),
        P("table", None, None, None),
        P("table", "section", None),
        P(("section", "table"), None, None),
        P(("section", "table"), None),
    )
    out_specs = P(("section", "table"), None)
    return jax.shard_map(
        per_device, mesh=mesh, in_specs=in_specs, out_specs=out_specs, check_vma=False
    )
```

```python
import jax
import jax.numpy as jnp
from jax import lax
from jax.experimental import pallas as pl
from jax.experimental.pallas import tpu as pltpu
from jax.sharding import PartitionSpec as P

BF = jnp.bfloat16
F32 = jnp.float32
NT = (((1,), (1,)), ((), ()))
TN = (((0,), (0,)), ((), ()))
EPSILON = 1e-05
DECAY_WEIGHT = 0.5
MICRO_ROWS = 64


def gather_rows(table, ids):
    rows, width = table.shape
    count = ids.shape[0]
    block = 1024
    chunk = 128

    def body(idx, tab, out, wide, tmp):
        step = pl.program_id(0)

        @pl.when(step == 0)
        def _():
            wide[...] = tab[...].astype(F32)

        @pl.loop(0, block // chunk)
        def _(part):
            base = step * block + part * chunk
            for j in range(chunk):
                tmp[pl.ds(j, 1), :] = wide[pl.ds(idx[base + j], 1), :]
            out[pl.ds(pl.multiple_of(part * chunk, chunk), chunk), :] = tmp[...].astype(BF)

    return pl.pallas_call(
        body,
        grid=(count // block,),
        in_specs=[
            pl.BlockSpec(memory_space=pltpu.SMEM),
            pl.BlockSpec((rows, width), lambda i: (0, 0)),
        ],
        out_specs=pl.BlockSpec((block, width), lambda i: (i, 0)),
        out_shape=jax.ShapeDtypeStruct((count, width), BF),
        scratch_shapes=[pltpu.VMEM((rows, width), F32), pltpu.VMEM((chunk, width), F32)],
        cost_estimate=pl.CostEstimate(flops=count * width, bytes_accessed=8 << 20, transcendentals=0),
        name="gather_rows",
    )(ids, table)


def scatter_rows(values, ids, rows, before=None):
    count, width = values.shape
    extra = [] if before is None else [before]
    block = 1024
    group = 16

    def body(idx, val, *refs):
        out, acc, wide, sem = refs[-4:]
        step = pl.program_id(0)

        @pl.when(step == 0)
        def _():
            if before is None:
                acc[...] = jnp.zeros_like(acc)
            else:
                acc[pl.ds(rows, 8), :] = jnp.zeros((8, width), F32)
                start = pltpu.make_async_copy(refs[0], acc.at[pl.ds(0, rows), :], sem)
                start.start()
                start.wait()

        wide[...] = val[...].astype(F32)

        @pl.loop(0, block // (4 * group))
        def _(part):
            for sub in range(4):
                at = part * (4 * group) + sub * group
                base = step * block + at
                where = [idx[base + j] for j in range(group)]
                new = [
                    acc[pl.ds(where[j], 1), :] + wide[pl.ds(at + j, 1), :]
                    for j in range(group)
                ]
                for j in range(group):
                    acc[pl.ds(where[j], 1), :] = new[j]

        @pl.when(step == pl.num_programs(0) - 1)
        def _():
            copy = pltpu.make_async_copy(acc.at[pl.ds(0, rows), :], out, sem)
            copy.start()
            copy.wait()

    return pl.pallas_call(
        body,
        grid=(count // block,),
        in_specs=[
            pl.BlockSpec(memory_space=pltpu.SMEM),
            pl.BlockSpec((block, width), lambda i: (i, 0)),
        ] + [pl.BlockSpec(memory_space=pl.ANY)] * len(extra),
        out_specs=pl.BlockSpec(memory_space=pl.ANY),
        out_shape=jax.ShapeDtypeStruct((rows, width), F32),
        scratch_shapes=[
            pltpu.VMEM((rows + 8, width), F32),
            pltpu.VMEM((block, width), F32),
            pltpu.SemaphoreType.DMA,
        ],
        cost_estimate=pl.CostEstimate(flops=count * width, bytes_accessed=16 << 20, transcendentals=0),
        name="scatter_rows",
    )(ids, values, *extra)


def lookup_matrix(slots, lcb, owners, cap):
    samples, features = slots.shape
    embeds = lcb.shape[0]
    shift = cap.bit_length() - 1
    half = cap // 2
    pairs = owners // 2

    def body(slot_ref, lcb_ref, out_ref):
        tiled = jnp.concatenate([lcb_ref[...].astype(F32)] * 2, axis=0).astype(BF)
        zero = jnp.zeros((), BF)
        lane = lax.broadcasted_iota(jnp.int32, (2 * cap, features), 0)
        row = (lax.broadcasted_iota(jnp.int32, (16, features), 0) // embeds).astype(F32).astype(BF)
        parts = []
        for h in range(2):
            slot = slot_ref[0, pl.ds(h, 1), :]
            pair = lax.shift_right_logical(slot, shift + 1)
            odd = lax.shift_right_logical(slot, shift) & 1
            col = slot & (cap - 1)
            place = lax.shift_right_logical(col, shift - 1) * cap + odd * half + (col & (half - 1))
            picks = jnp.where(lane == place, 1.0, 0.0).astype(BF)
            pair16 = jnp.broadcast_to(pair.astype(F32), (16, features)).astype(BF)
            rows = []
            for o in range(0, pairs, 2):
                rows.append(jnp.where(pair16 == row + jnp.asarray(float(o), BF), tiled, zero))
            spread = jnp.concatenate(rows, axis=0)
            got = lax.dot_general(spread, picks, NT, preferred_element_type=F32)
            parts.append(got.reshape(pairs, embeds, 2 * cap))
        out_ref[...] = jnp.concatenate(parts, axis=1).astype(BF)

    return pl.pallas_call(
        body,
        grid=(samples // 2,),
        in_specs=[
            pl.BlockSpec((1, 2, features), lambda i: (i, 0, 0)),
            pl.BlockSpec((embeds, features), lambda i: (0, 0)),
        ],
        out_specs=pl.BlockSpec((pairs, 2 * embeds, 2 * cap), lambda i: (0, i, 0)),
        out_shape=jax.ShapeDtypeStruct((pairs, samples * embeds, 2 * cap), BF),
        cost_estimate=pl.CostEstimate(
            flops=2 * samples * owners * embeds * cap * features, bytes_accessed=16 << 20, transcendentals=0
        ),
        name="lookup_matrix",
    )(slots.reshape(samples // 2, 2, features), lcb)


def compress(matrix, halves):
    pairs, outs, slots = matrix.shape
    width = halves[0].shape[1]
    part = slots // 2
    step_pairs = 8
    embeds = 8

    def half_sum(h, before):
        def body(mat, rows, *refs):
            out = refs[-1]
            step = pl.program_id(0)

            @pl.when(step == 0)
            def _():
                out[...] = jnp.zeros_like(out) if before is None else refs[0][...]

            total = out[...]
            for i in range(step_pairs):
                total += jnp.dot(mat[i], rows[pl.ds(i * part, part), :], preferred_element_type=F32)
            out[...] = total

        extra = [] if before is None else [before]
        return pl.pallas_call(
            body,
            grid=(pairs // step_pairs,),
            in_specs=[
                pl.BlockSpec((step_pairs, outs, part), lambda i: (i, 0, h)),
                pl.BlockSpec((step_pairs * part, width), lambda i: (i, 0)),
            ] + [pl.BlockSpec((outs, width), lambda i: (0, 0))] * len(extra),
            out_specs=pl.BlockSpec((outs, width), lambda i: (0, 0)),
            out_shape=jax.ShapeDtypeStruct((outs, width), F32),
            cost_estimate=pl.CostEstimate(flops=2 * outs * pairs * part * width, bytes_accessed=6 << 20, transcendentals=0),
            name="compress",
        )(matrix, halves[h], *extra)

    return half_sum(1, half_sum(0, None))


def expand(matrix, grads, rows, decay, h):
    pairs, outs, slots = matrix.shape
    width = rows.shape[1]
    part = slots // 2
    step_pairs = 8
    samples, model = grads.shape
    embeds = model // width

    def body(mat, grad, rows_ref, out, wide, tall):
        @pl.when(pl.program_id(0) == 0)
        def _():
            for k in range(embeds):
                wide[pl.ds(k, samples, stride=embeds), :] = grad[:, k * width : (k + 1) * width].astype(F32)
            tall[...] = wide[...].astype(BF)

        for i in range(step_pairs):
            at = pl.ds(i * part, part)
            got = lax.dot_general(mat[i], tall[...], TN, preferred_element_type=F32)
            out[at, :] = (got + decay * rows_ref[at, :].astype(F32)).astype(BF)

    return pl.pallas_call(
        body,
        grid=(pairs // step_pairs,),
        in_specs=[
            pl.BlockSpec((step_pairs, outs, part), lambda i: (i, 0, h)),
            pl.BlockSpec((samples, model), lambda i: (0, 0)),
            pl.BlockSpec((step_pairs * part, width), lambda i: (i, 0)),
        ],
        out_specs=pl.BlockSpec((step_pairs * part, width), lambda i: (i, 0)),
        out_shape=jax.ShapeDtypeStruct((pairs * part, width), BF),
        scratch_shapes=[pltpu.VMEM((outs, width), F32), pltpu.VMEM((outs, width), BF)],
        cost_estimate=pl.CostEstimate(flops=2 * outs * pairs * part * width, bytes_accessed=8 << 20, transcendentals=0),
        name="expand",
    )(matrix, grads, rows)


def layer_forward(a_ref, mix, gain, w_up, w_down, keep, out_ref, last, ready, send):
    interact, inv_keep, hidden, prod, normed = keep
    rows, model = a_ref.shape
    width = mix.shape[1]
    embeds = model // width
    inner = w_up.shape[1]
    cols = [slice(k * width, (k + 1) * width) for k in range(embeds)]
    for k in range(embeds):
        for q in range(k, embeds):
            both = a_ref[:, cols[k]] * a_ref[:, cols[q]]
            prod[k * rows : (k + 1) * rows, cols[q]] = both
            if q > k:
                prod[q * rows : (q + 1) * rows, cols[k]] = both
    interact[...] = jnp.dot(prod[...], mix[...], preferred_element_type=F32)
    square = None
    for k in range(embeds):
        part = interact[k * rows : (k + 1) * rows, :]
        square = part * part if square is None else square + part * part
    inv = lax.rsqrt(jnp.sum(square, axis=1, keepdims=True) * (1.0 / model) + EPSILON)
    inv_keep[...] = jnp.broadcast_to(inv, (rows, width))
    for k in range(embeds):
        part = interact[k * rows : (k + 1) * rows, :]
        normed[:, cols[k]] = (part * inv * gain[:, cols[k]]).astype(BF)
    tile = min(512, inner)
    for n in range(0, inner, tile):
        before = jnp.dot(normed[...], w_up[:, n : n + tile], preferred_element_type=F32)
        hidden[:, n : n + tile] = jnp.maximum(before, 0.0).astype(BF)
    ready()

    @pl.when(jnp.logical_not(last))
    def _():
        tile = 256
        for n in range(0, model, tile):
            got = jnp.dot(hidden[...], w_down[:, n : n + tile], preferred_element_type=F32)
            out_ref[:, n : n + tile] = (got + a_ref[:, n : n + tile].astype(F32)).astype(BF)
            send(n, tile)


def layer_backward(a_ref, g_ref, unmix, gain, up_t, down_t, keep, gated, unit, pulled, spread, out_ref, send):
    interact, inv_keep, hidden, prod, normed = keep
    rows, model = a_ref.shape
    width = unmix.shape[0]
    embeds = model // width
    inner = down_t.shape[1]
    cols = [slice(k * width, (k + 1) * width) for k in range(embeds)]
    tile = min(512, inner)
    for n in range(0, inner, tile):
        up = jnp.dot(g_ref[...], down_t[:, n : n + tile], preferred_element_type=F32)
        gated[:, n : n + tile] = jnp.where(hidden[:, n : n + tile].astype(F32) > 0.0, up, 0.0).astype(BF)
    tile = 256
    cross = None
    for n in range(0, model, tile):
        got = jnp.dot(gated[...], up_t[:, n : n + tile], preferred_element_type=F32)
        got = got * gain[:, n : n + tile]
        unit[:, n : n + tile] = got
        for k in range(n // width, (n + tile) // width):
            part = got[:, k * width - n : (k + 1) * width - n] * interact[k * rows : (k + 1) * rows, :]
            cross = part if cross is None else cross + part
    mean = jnp.sum(cross, axis=1, keepdims=True) * (1.0 / model)
    inv = inv_keep[...]
    slope = inv * inv * mean
    for k in range(embeds):
        part = inv * (unit[:, cols[k]] - interact[k * rows : (k + 1) * rows, :] * slope)
        pulled[k * rows : (k + 1) * rows, :] = part.astype(BF)
    for q in range(0, embeds, 2):
        both = slice(q * width, (q + 2) * width)
        spread[:, both] = jnp.dot(pulled[...], unmix[:, both], preferred_element_type=F32)
    part_rows = 16
    for b in range(0, rows, part_rows):
        here = pl.ds(b, part_rows)
        a = [a_ref[here, cols[k]].astype(F32) for k in range(embeds)]
        total = [g_ref[here, cols[k]].astype(F32) for k in range(embeds)]
        for k in range(embeds):
            for q in range(k, embeds):
                pair = spread[pl.ds(k * rows + b, part_rows), cols[q]] + spread[pl.ds(q * rows + b, part_rows), cols[k]]
                total[k] = total[k] + pair * a[q]
                if q > k:
                    total[q] = total[q] + pair * a[k]
        for k in range(embeds):
            out_ref[here, cols[k]] = total[k].astype(BF)
        if (b + part_rows) % 32 == 0:
            send((b + part_rows) // 32 - 1)


def layer_pipeline(shares, top, mix, unmix, gain, w_up, w_down, up_t, down_t, stages, rows):
    look, model = shares.shape
    micro = top.shape[0] // rows
    per = rows // look
    inner = w_up.shape[1]
    width = mix.shape[1]
    embeds = model // width
    chunks = model // 256
    copy_to = pltpu.make_async_remote_copy
    copy_here = pltpu.make_async_copy

    def body(
        share_in, top_in, mix_ref, unmix_ref, gain_ref, up_in, down_in, up_t_in, down_t_in, out,
        acts, cots, acts_out, cots_out, share, up_v, down_v, up_tv, down_tv,
        interact, inv_keep, hidden, prod, normed, gated, unit, pulled, spread,
        wsem, tsem, fsend, frecv, gsend, grecv, isend, irecv, osend, orecv, lsem,
    ):
        me = lax.axis_index("section")
        first, last = me == 0, me == stages - 1
        loads = [
            copy_here(src, dst, wsem.at[i])
            for i, (src, dst) in enumerate(
                [(up_in, up_v), (down_in, down_v), (down_t_in, down_tv), (up_t_in, up_tv)]
            )
        ]
        loads[0].start()
        loads[1].start()
        tops = [copy_here(top_in.at[pl.ds(m * rows, rows), :], cots.at[m], tsem.at[m]) for m in range(micro)]

        @pl.when(last)
        def _():
            for m in range(micro):
                tops[m].start()

        barrier = pltpu.get_barrier_semaphore()
        for d in range(1, stages):
            pl.semaphore_signal(
                barrier, inc=1, device_id={"section": lax.rem(me + d, stages)},
                device_id_type=pl.DeviceIdType.MESH,
            )
        pl.semaphore_wait(barrier, stages - 1)

        def entry(section):
            slot, off = section // per, lax.rem(section, per) * look
            return copy_to(
                src_ref=share_in, dst_ref=acts.at[slot, pl.ds(pl.multiple_of(off, look), look), :],
                send_sem=isend, recv_sem=irecv.at[section],
                device_id={"section": 0}, device_id_type=pl.DeviceIdType.MESH,
            )

        own = copy_here(share_in, acts.at[0, pl.ds(0, look), :], irecv.at[0])

        @pl.when(first)
        def _():
            own.start()
            own.wait()
            for section in range(1, stages):
                entry(jnp.int32(section)).wait_recv()

        @pl.when(jnp.logical_not(first))
        def _():
            entry(me).start()

        def onward(m, c):
            piece = pl.ds(c * 256, 256)
            return copy_to(
                src_ref=acts_out.at[m, :, piece], dst_ref=acts.at[m, :, piece],
                send_sem=fsend.at[m, c], recv_sem=frecv.at[m, c],
                device_id={"section": lax.rem(me + 1, stages)}, device_id_type=pl.DeviceIdType.MESH,
            )

        def back(m, j):
            piece = pl.ds(j * look, look)
            return copy_to(
                src_ref=cots_out.at[m, piece, :], dst_ref=cots.at[m, piece, :],
                send_sem=gsend.at[m, j], recv_sem=grecv.at[m, j],
                device_id={"section": lax.rem(me + stages - 1, stages)}, device_id_type=pl.DeviceIdType.MESH,
            )

        def leave(m, j, section):
            return copy_to(
                src_ref=cots_out.at[m, pl.ds(j * look, look), :], dst_ref=share,
                send_sem=osend.at[section], recv_sem=orecv,
                device_id={"section": section}, device_id_type=pl.DeviceIdType.MESH,
            )

        keep_own = copy_here(cots_out.at[0, pl.ds(0, look), :], share, lsem)
        loads[0].wait()

        def step(i, carry):
            ahead = jnp.where(last, lax.rem(i, 2) == 0, i < micro)
            m = jnp.where(last, i // 2, lax.rem(i, micro))
            keep = (interact.at[m], inv_keep.at[m], hidden.at[m], prod, normed)

            @pl.when(ahead)
            def _():
                @pl.when(jnp.logical_not(first))
                def _():
                    for c in range(chunks):
                        onward(m, c).wait_recv()

                def ready():
                    @pl.when(i == 0)
                    def _():
                        loads[1].wait()
                        loads[2].start()
                        loads[3].start()

                layer_forward(
                    acts.at[m], mix_ref, gain_ref, up_v, down_v, keep, acts_out.at[m], last, ready,
                    lambda n, tile: onward(m, n // 256).start(),
                )

            @pl.when(jnp.logical_not(ahead))
            def _():
                @pl.when(m == 0)
                def _():
                    loads[2].wait()
                    loads[3].wait()

                @pl.when(last)
                def _():
                    copy_here(top_in.at[pl.ds(pl.multiple_of(m * rows, rows), rows), :], cots.at[m], tsem.at[m]).wait()

                @pl.when(jnp.logical_not(last))
                def _():
                    for j in range(per):
                        back(m, j).wait_recv()

                def send(j):
                    @pl.when(jnp.logical_not(first))
                    def _():
                        back(m, j).start()

                    @pl.when(first)
                    def _():
                        section = m * per + j
                        if j == 0:
                            @pl.when(section == 0)
                            def _():
                                keep_own.start()

                            @pl.when(section > 0)
                            def _():
                                leave(m, j, section).start()
                        else:
                            leave(m, j, section).start()

                layer_backward(
                    acts.at[m], cots.at[m], unmix_ref, gain_ref, up_tv, down_tv, keep,
                    gated, unit, pulled, spread, cots_out.at[m], send,
                )

            return carry

        lax.fori_loop(0, 2 * micro, step, 0)

        @pl.when(first)
        def _():
            keep_own.wait()
            for section in range(1, stages):
                leave(section // per, section % per, jnp.int32(section)).wait_send()

        @pl.when(jnp.logical_not(first))
        def _():
            leave(0, 0, jnp.int32(0)).wait_recv()
            entry(me).wait_send()
            for m in range(micro):
                for j in range(per):
                    back(m, j).wait_send()

        @pl.when(jnp.logical_not(last))
        def _():
            for m in range(micro):
                for c in range(chunks):
                    onward(m, c).wait_send()

        out[...] = share[...]

    vmem = pl.BlockSpec(memory_space=pltpu.VMEM)
    hbm = pl.BlockSpec(memory_space=pl.ANY)
    dma = pltpu.SemaphoreType.DMA
    block = (micro, rows, model)
    tall = embeds * rows
    return pl.pallas_call(
        body,
        in_specs=[vmem, hbm, vmem, vmem, vmem, hbm, hbm, hbm, hbm],
        out_specs=vmem,
        out_shape=jax.ShapeDtypeStruct((look, model), BF),
        scratch_shapes=[
            pltpu.VMEM(block, BF), pltpu.VMEM(block, BF), pltpu.VMEM(block, BF), pltpu.VMEM(block, BF),
            pltpu.VMEM((look, model), BF),
            pltpu.VMEM((model, inner), BF), pltpu.VMEM((inner, model), BF),
            pltpu.VMEM((inner, model), BF), pltpu.VMEM((model, inner), BF),
            pltpu.VMEM((micro, tall, width), F32), pltpu.VMEM((micro, rows, width), F32),
            pltpu.VMEM((micro, rows, inner), BF),
            pltpu.VMEM((tall, model), BF), pltpu.VMEM((rows, model), BF), pltpu.VMEM((rows, inner), BF),
            pltpu.VMEM((rows, model), F32), pltpu.VMEM((tall, width), BF), pltpu.VMEM((tall, model), F32),
            dma((4,)), dma((micro,)), dma((micro, chunks)), dma((micro, chunks)),
            dma((micro, per)), dma((micro, per)),
            dma, dma((stages,)), dma((stages,)), dma, dma,
        ],
        compiler_params=pltpu.CompilerParams(
            collective_id=0, has_side_effects=True, vmem_limit_bytes=60 << 20
        ),
        name="layer_pipeline",
    )(shares, top, mix, unmix, gain, w_up, w_down, up_t, down_t)


def mixers(proj):
    embeds, width = proj.shape
    mix = jnp.broadcast_to(proj[:, None, :], (embeds, width, width)).reshape(embeds * width, width)
    unmix = jnp.broadcast_to(proj.T[:, :, None], (width, embeds, width)).reshape(width, embeds * width)
    return mix, unmix


def per_device(
    emb_table,
    lcb_weight,
    fm_proj,
    norm_gain,
    w_up,
    w_down,
    top_grad,
    lookup_slot,
    wanted_rows,
    row_counts,
):
    section_count = lax.axis_size("section")
    owners = section_count * lax.axis_size("table")
    cap = wanted_rows.shape[2]
    rows_here, embed_width = emb_table.shape
    picked_rows = wanted_rows[0]

    half = cap // 2

    def exchange(rows):
        rows = rows.reshape(owners, half, embed_width)
        rows = lax.all_to_all(rows, ("section", "table"), split_axis=0, concat_axis=0, tiled=True)
        return rows.reshape(owners * half, embed_width)

    def halves(ids):
        return [ids[:, h * half : (h + 1) * half].reshape(-1) for h in range(2)]

    fetched = [exchange(gather_rows(emb_table, ids)) for ids in halves(picked_rows)]
    lookup_slots = lookup_slot[0]
    look_dev = lookup_slots.shape[0]
    model_width = top_grad.shape[3]
    matrix = lookup_matrix(lookup_slots, lcb_weight, owners, cap)
    shares = compress(matrix, fetched).astype(BF).reshape(look_dev, -1)
    mix, unmix = mixers(fm_proj[0])
    lead_share = layer_pipeline(
        shares,
        top_grad.reshape(-1, model_width),
        mix,
        unmix,
        norm_gain.astype(F32),
        w_up[0],
        w_down[0],
        w_up[0].T,
        w_down[0].T,
        section_count,
        MICRO_ROWS,
    )
    live_slots = jnp.arange(cap)[None, :] < row_counts[0][:, None]
    targets = halves(jnp.where(live_slots, picked_rows, rows_here))
    returned = [exchange(expand(matrix, lead_share, fetched[h], DECAY_WEIGHT, h)) for h in range(2)]
    table_grad = scatter_rows(returned[0], targets[0], rows_here)
    return scatter_rows(returned[1], targets[1], rows_here, table_grad)


def solution(mesh):
    in_specs = (
        P(("section", "table"), None),
        P(),
        P("section", None, None),
        P("section", None),
        P("section", None, None),
        P("section", None, None),
        P("table", None, None, None),
        P("table", "section", None),
        P(("section", "table"), None, None),
        P(("section", "table"), None),
    )
    out_specs = P(("section", "table"), None)
    return jax.shard_map(
        per_device, mesh=mesh, in_specs=in_specs, out_specs=out_specs, check_vma=False
    )
```

```python
import jax
import jax.numpy as jnp
from jax import lax
from jax.experimental import pallas as pl
from jax.experimental.pallas import tpu as pltpu
from jax.sharding import PartitionSpec as P

BF = jnp.bfloat16
F32 = jnp.float32
NT = (((1,), (1,)), ((), ()))
TN = (((0,), (0,)), ((), ()))
EPSILON = 1e-05
DECAY_WEIGHT = 0.5
MICRO_ROWS = 128
CHUNK = 512


def gather_rows(table, ids):
    rows, width = table.shape
    count = ids.shape[0]
    block = 1024
    chunk = 128

    def body(idx, tab, out, wide, tmp):
        step = pl.program_id(0)

        @pl.when(step == 0)
        def _():
            wide[...] = tab[...].astype(F32)

        @pl.loop(0, block // chunk)
        def _(part):
            base = step * block + part * chunk
            for j in range(chunk):
                tmp[pl.ds(j, 1), :] = wide[pl.ds(idx[base + j], 1), :]
            out[pl.ds(pl.multiple_of(part * chunk, chunk), chunk), :] = tmp[...].astype(BF)

    return pl.pallas_call(
        body,
        grid=(count // block,),
        in_specs=[
            pl.BlockSpec(memory_space=pltpu.SMEM),
            pl.BlockSpec((rows, width), lambda i: (0, 0)),
        ],
        out_specs=pl.BlockSpec((block, width), lambda i: (i, 0)),
        out_shape=jax.ShapeDtypeStruct((count, width), BF),
        scratch_shapes=[pltpu.VMEM((rows, width), F32), pltpu.VMEM((chunk, width), F32)],
        cost_estimate=pl.CostEstimate(flops=count * width, bytes_accessed=8 << 20, transcendentals=0),
        name="gather_rows",
    )(ids, table)


def scatter_rows(values, ids, rows, before=None):
    count, width = values.shape
    extra = [] if before is None else [before]
    block = 1024
    group = 16

    def body(idx, val, *refs):
        out, acc, wide, sem = refs[-4:]
        step = pl.program_id(0)

        @pl.when(step == 0)
        def _():
            if before is None:
                acc[...] = jnp.zeros_like(acc)
            else:
                acc[pl.ds(rows, 8), :] = jnp.zeros((8, width), F32)
                start = pltpu.make_async_copy(refs[0], acc.at[pl.ds(0, rows), :], sem)
                start.start()
                start.wait()

        wide[...] = val[...].astype(F32)

        @pl.loop(0, block // (4 * group))
        def _(part):
            for sub in range(4):
                at = part * (4 * group) + sub * group
                base = step * block + at
                where = [idx[base + j] for j in range(group)]
                new = [
                    acc[pl.ds(where[j], 1), :] + wide[pl.ds(at + j, 1), :]
                    for j in range(group)
                ]
                for j in range(group):
                    acc[pl.ds(where[j], 1), :] = new[j]

        @pl.when(step == pl.num_programs(0) - 1)
        def _():
            copy = pltpu.make_async_copy(acc.at[pl.ds(0, rows), :], out, sem)
            copy.start()
            copy.wait()

    return pl.pallas_call(
        body,
        grid=(count // block,),
        in_specs=[
            pl.BlockSpec(memory_space=pltpu.SMEM),
            pl.BlockSpec((block, width), lambda i: (i, 0)),
        ] + [pl.BlockSpec(memory_space=pl.ANY)] * len(extra),
        out_specs=pl.BlockSpec(memory_space=pl.ANY),
        out_shape=jax.ShapeDtypeStruct((rows, width), F32),
        scratch_shapes=[
            pltpu.VMEM((rows + 8, width), F32),
            pltpu.VMEM((block, width), F32),
            pltpu.SemaphoreType.DMA,
        ],
        cost_estimate=pl.CostEstimate(flops=count * width, bytes_accessed=16 << 20, transcendentals=0),
        name="scatter_rows",
    )(ids, values, *extra)


def lookup_matrix(slots, lcb, owners, cap):
    samples, features = slots.shape
    embeds = lcb.shape[0]
    shift = cap.bit_length() - 1
    pairs = owners // 2

    def body(slot_ref, lcb_ref, out_ref):
        tiled = jnp.concatenate([lcb_ref[...].astype(F32)] * 2, axis=0).astype(BF)
        zero = jnp.zeros((), BF)
        lane = lax.broadcasted_iota(jnp.int32, (2 * cap, features), 0)
        row = (lax.broadcasted_iota(jnp.int32, (16, features), 0) // embeds).astype(F32).astype(BF)
        parts = []
        for h in range(2):
            slot = slot_ref[0, pl.ds(h, 1), :]
            pair = lax.shift_right_logical(slot, shift + 1)
            place = slot & (2 * cap - 1)
            picks = jnp.where(lane == place, 1.0, 0.0).astype(BF)
            pair16 = jnp.broadcast_to(pair.astype(F32), (16, features)).astype(BF)
            rows = []
            for o in range(0, pairs, 2):
                rows.append(jnp.where(pair16 == row + jnp.asarray(float(o), BF), tiled, zero))
            spread = jnp.concatenate(rows, axis=0)
            got = lax.dot_general(spread, picks, NT, preferred_element_type=F32)
            parts.append(got.reshape(pairs, embeds, 2 * cap))
        out_ref[...] = jnp.concatenate(parts, axis=1).astype(BF)

    return pl.pallas_call(
        body,
        grid=(samples // 2,),
        in_specs=[
            pl.BlockSpec((1, 2, features), lambda i: (i, 0, 0)),
            pl.BlockSpec((embeds, features), lambda i: (0, 0)),
        ],
        out_specs=pl.BlockSpec((pairs, 2 * embeds, 2 * cap), lambda i: (0, i, 0)),
        out_shape=jax.ShapeDtypeStruct((pairs, samples * embeds, 2 * cap), BF),
        cost_estimate=pl.CostEstimate(
            flops=2 * samples * owners * embeds * cap * features, bytes_accessed=16 << 20, transcendentals=0
        ),
        name="lookup_matrix",
    )(slots.reshape(samples // 2, 2, features), lcb)


def compress(matrix, fetched, embeds):
    pairs, outs, slots = matrix.shape
    width = fetched.shape[1]
    samples = outs // embeds
    step_pairs = 8

    def body(mat, rows, out, acc):
        step = pl.program_id(0)

        @pl.when(step == 0)
        def _():
            acc[...] = jnp.zeros_like(acc)

        total = acc[...]
        for i in range(step_pairs):
            total += jnp.dot(mat[i], rows[pl.ds(i * slots, slots), :], preferred_element_type=F32)
        acc[...] = total

        @pl.when(step == pl.num_programs(0) - 1)
        def _():
            for k in range(embeds):
                out[:, k * width : (k + 1) * width] = acc[pl.ds(k, samples, stride=embeds), :].astype(BF)

    return pl.pallas_call(
        body,
        grid=(pairs // step_pairs,),
        in_specs=[
            pl.BlockSpec((step_pairs, outs, slots), lambda i: (i, 0, 0)),
            pl.BlockSpec((step_pairs * slots, width), lambda i: (i, 0)),
        ],
        out_specs=pl.BlockSpec((samples, embeds * width), lambda i: (0, 0)),
        out_shape=jax.ShapeDtypeStruct((samples, embeds * width), BF),
        scratch_shapes=[pltpu.VMEM((outs, width), F32)],
        name="compress",
    )(matrix, fetched)


def expand(matrix, grads, rows, decay):
    pairs, outs, slots = matrix.shape
    width = rows.shape[1]
    part = slots
    step_pairs = 8
    samples, model = grads.shape
    embeds = model // width

    def body(mat, grad, rows_ref, out, wide, tall):
        @pl.when(pl.program_id(0) == 0)
        def _():
            for k in range(embeds):
                wide[pl.ds(k, samples, stride=embeds), :] = grad[:, k * width : (k + 1) * width].astype(F32)
            tall[...] = wide[...].astype(BF)

        for i in range(step_pairs):
            at = pl.ds(i * part, part)
            got = lax.dot_general(mat[i], tall[...], TN, preferred_element_type=F32)
            out[at, :] = (got + decay * rows_ref[at, :].astype(F32)).astype(BF)

    return pl.pallas_call(
        body,
        grid=(pairs // step_pairs,),
        in_specs=[
            pl.BlockSpec((step_pairs, outs, part), lambda i: (i, 0, 0)),
            pl.BlockSpec((samples, model), lambda i: (0, 0)),
            pl.BlockSpec((step_pairs * part, width), lambda i: (i, 0)),
        ],
        out_specs=pl.BlockSpec((step_pairs * part, width), lambda i: (i, 0)),
        out_shape=jax.ShapeDtypeStruct((pairs * part, width), BF),
        scratch_shapes=[pltpu.VMEM((outs, width), F32), pltpu.VMEM((outs, width), BF)],
        cost_estimate=pl.CostEstimate(flops=2 * outs * pairs * part * width, bytes_accessed=8 << 20, transcendentals=0),
        name="expand",
    )(matrix, grads, rows)


def layer_forward(a_ref, mix, gain, w_up, w_down, keep, out_ref, last, ready, send):
    interact, inv_keep, hidden, prod, normed = keep
    rows, model = a_ref.shape
    width = mix.shape[1]
    embeds = model // width
    inner = w_up.shape[1]
    cols = [slice(k * width, (k + 1) * width) for k in range(embeds)]
    for k in range(embeds):
        for q in range(k, embeds):
            both = a_ref[:, cols[k]] * a_ref[:, cols[q]]
            prod[k * rows : (k + 1) * rows, cols[q]] = both
            if q > k:
                prod[q * rows : (q + 1) * rows, cols[k]] = both
    interact[...] = jnp.dot(prod[...], mix[...], preferred_element_type=F32)
    square = None
    for k in range(embeds):
        part = interact[k * rows : (k + 1) * rows, :]
        square = part * part if square is None else square + part * part
    inv = lax.rsqrt(jnp.sum(square, axis=1, keepdims=True) * (1.0 / model) + EPSILON)
    inv_keep[...] = jnp.broadcast_to(inv, (rows, width))
    for k in range(embeds):
        part = interact[k * rows : (k + 1) * rows, :]
        normed[:, cols[k]] = (part * inv * gain[:, cols[k]]).astype(BF)
    tile = min(512, inner)
    for n in range(0, inner, tile):
        before = jnp.dot(normed[...], w_up[:, n : n + tile], preferred_element_type=F32)
        hidden[:, n : n + tile] = jnp.maximum(before, 0.0).astype(BF)
    ready()

    @pl.when(jnp.logical_not(last))
    def _():
        tile = 256
        for n in range(0, model, tile):
            got = jnp.dot(hidden[...], w_down[:, n : n + tile], preferred_element_type=F32)
            out_ref[:, n : n + tile] = (got + a_ref[:, n : n + tile].astype(F32)).astype(BF)
            send(n, tile)


def layer_backward(a_ref, g_ref, unmix, gain, up_t, down_t, keep, gated, unit, pulled, spread, out_ref, send):
    interact, inv_keep, hidden, prod, normed = keep
    rows, model = a_ref.shape
    width = unmix.shape[0]
    embeds = model // width
    inner = down_t.shape[1]
    cols = [slice(k * width, (k + 1) * width) for k in range(embeds)]
    tile = min(512, inner)
    for n in range(0, inner, tile):
        up = jnp.dot(g_ref[...], down_t[:, n : n + tile], preferred_element_type=F32)
        gated[:, n : n + tile] = jnp.where(hidden[:, n : n + tile].astype(F32) > 0.0, up, 0.0).astype(BF)
    tile = 256
    cross = None
    for n in range(0, model, tile):
        got = jnp.dot(gated[...], up_t[:, n : n + tile], preferred_element_type=F32)
        got = got * gain[:, n : n + tile]
        unit[:, n : n + tile] = got
        for k in range(n // width, (n + tile) // width):
            part = got[:, k * width - n : (k + 1) * width - n] * interact[k * rows : (k + 1) * rows, :]
            cross = part if cross is None else cross + part
    mean = jnp.sum(cross, axis=1, keepdims=True) * (1.0 / model)
    inv = inv_keep[...]
    slope = inv * inv * mean
    for k in range(embeds):
        part = inv * (unit[:, cols[k]] - interact[k * rows : (k + 1) * rows, :] * slope)
        pulled[k * rows : (k + 1) * rows, :] = part.astype(BF)
    for q in range(0, embeds, 2):
        both = slice(q * width, (q + 2) * width)
        spread[:, both] = jnp.dot(pulled[...], unmix[:, both], preferred_element_type=F32)
    part_rows = 16
    for b in range(0, rows, part_rows):
        here = pl.ds(b, part_rows)
        a = [a_ref[here, cols[k]].astype(F32) for k in range(embeds)]
        total = [g_ref[here, cols[k]].astype(F32) for k in range(embeds)]
        for k in range(embeds):
            for q in range(k, embeds):
                pair = spread[pl.ds(k * rows + b, part_rows), cols[q]] + spread[pl.ds(q * rows + b, part_rows), cols[k]]
                total[k] = total[k] + pair * a[q]
                if q > k:
                    total[q] = total[q] + pair * a[k]
        for k in range(embeds):
            out_ref[here, cols[k]] = total[k].astype(BF)
        if (b + part_rows) % 32 == 0:
            send((b + part_rows) // 32 - 1)


def layer_pipeline(shares, top, mix, unmix, gain, w_up, w_down, stages, rows):
    look, model = shares.shape
    micro = top.shape[0] // rows
    per = rows // look
    inner = w_up.shape[1]
    width = mix.shape[1]
    embeds = model // width
    chunks = model // CHUNK
    copy_to = pltpu.make_async_remote_copy
    copy_here = pltpu.make_async_copy

    def body(
        share_in, top_in, mix_ref, unmix_ref, gain_ref, up_in, down_in, out,
        acts, cots, acts_out, cots_out, share, up_v, down_v, up_tv, down_tv,
        interact, inv_keep, hidden, prod, normed, gated, unit, pulled, spread,
        wsem, tsem, fsend, frecv, gsend, grecv, isend, irecv, osend, orecv, lsem,
    ):
        me = lax.axis_index("section")
        first, last = me == 0, me == stages - 1
        loads = [
            copy_here(src, dst, wsem.at[i])
            for i, (src, dst) in enumerate(
                [(up_in, up_v), (down_in, down_v)]
            )
        ]
        loads[0].start()
        loads[1].start()
        tops = [copy_here(top_in.at[pl.ds(m * rows, rows), :], cots.at[m], tsem.at[m]) for m in range(micro)]

        @pl.when(last)
        def _():
            for m in range(micro):
                tops[m].start()

        barrier = pltpu.get_barrier_semaphore()
        for d in range(1, stages):
            pl.semaphore_signal(
                barrier, inc=1, device_id={"section": lax.rem(me + d, stages)},
                device_id_type=pl.DeviceIdType.MESH,
            )
        pl.semaphore_wait(barrier, stages - 1)

        def entry(section):
            slot, off = section // per, lax.rem(section, per) * look
            return copy_to(
                src_ref=share_in, dst_ref=acts.at[slot, pl.ds(pl.multiple_of(off, look), look), :],
                send_sem=isend, recv_sem=irecv.at[section],
                device_id={"section": 0}, device_id_type=pl.DeviceIdType.MESH,
            )

        own = copy_here(share_in, acts.at[0, pl.ds(0, look), :], irecv.at[0])

        @pl.when(first)
        def _():
            own.start()
            own.wait()

        @pl.when(jnp.logical_not(first))
        def _():
            entry(me).start()

        def onward(m, c):
            piece = pl.ds(c * CHUNK, CHUNK)
            return copy_to(
                src_ref=acts_out.at[m, :, piece], dst_ref=acts.at[m, :, piece],
                send_sem=fsend.at[m, c], recv_sem=frecv.at[m, c],
                device_id={"section": lax.rem(me + 1, stages)}, device_id_type=pl.DeviceIdType.MESH,
            )

        def back(m, j):
            piece = pl.ds(j * look, look)
            return copy_to(
                src_ref=cots_out.at[m, piece, :], dst_ref=cots.at[m, piece, :],
                send_sem=gsend.at[m, j], recv_sem=grecv.at[m, j],
                device_id={"section": lax.rem(me + stages - 1, stages)}, device_id_type=pl.DeviceIdType.MESH,
            )

        def leave(m, j, section):
            return copy_to(
                src_ref=cots_out.at[m, pl.ds(j * look, look), :], dst_ref=share,
                send_sem=osend.at[section], recv_sem=orecv,
                device_id={"section": section}, device_id_type=pl.DeviceIdType.MESH,
            )

        keep_own = copy_here(cots_out.at[0, pl.ds(0, look), :], share, lsem)
        loads[0].wait()
        late = me > stages // 2

        def turn():
            tile = 256

            @pl.loop(0, inner // tile)
            def _(n):
                at = pl.ds(pl.multiple_of(n * tile, tile), tile)
                up_tv[at, :] = up_v[:, at].T
                down_tv[:, at] = down_v[at, :].T

        @pl.when(late)
        def _():
            loads[1].wait()
            turn()

        def step(i, carry):
            ahead = jnp.where(last, lax.rem(i, 2) == 0, i < micro)
            m = jnp.where(last, i // 2, lax.rem(i, micro))
            keep = (interact.at[m], inv_keep.at[m], hidden.at[m], prod, normed)

            @pl.when(ahead)
            def _():
                @pl.when(jnp.logical_not(first))
                def _():
                    for c in range(chunks):
                        onward(m, c).wait_recv()

                @pl.when(first)
                def _():
                    for j in range(per):
                        @pl.when(m * per + j > 0)
                        def _():
                            entry(m * per + j).wait_recv()

                def ready():
                    @pl.when((i == 0) & jnp.logical_not(late))
                    def _():
                        loads[1].wait()

                layer_forward(
                    acts.at[m], mix_ref, gain_ref, up_v, down_v, keep, acts_out.at[m], last, ready,
                    lambda n, tile: onward(m, n // CHUNK).start() if (n + tile) % CHUNK == 0 else None,
                )

            @pl.when(jnp.logical_not(ahead))
            def _():
                @pl.when((m == 0) & jnp.logical_not(late))
                def _():
                    turn()

                @pl.when(last)
                def _():
                    copy_here(top_in.at[pl.ds(pl.multiple_of(m * rows, rows), rows), :], cots.at[m], tsem.at[m]).wait()

                @pl.when(jnp.logical_not(last))
                def _():
                    for j in range(per):
                        back(m, j).wait_recv()

                def send(j):
                    @pl.when(jnp.logical_not(first))
                    def _():
                        back(m, j).start()

                    @pl.when(first)
                    def _():
                        section = m * per + j
                        if j == 0:
                            @pl.when(section == 0)
                            def _():
                                keep_own.start()

                            @pl.when(section > 0)
                            def _():
                                leave(m, j, section).start()
                        else:
                            leave(m, j, section).start()

                layer_backward(
                    acts.at[m], cots.at[m], unmix_ref, gain_ref, up_tv, down_tv, keep,
                    gated, unit, pulled, spread, cots_out.at[m], send,
                )

            return carry

        lax.fori_loop(0, 2 * micro, step, 0)

        @pl.when(first)
        def _():
            keep_own.wait()
            for section in range(1, stages):
                leave(section // per, section % per, jnp.int32(section)).wait_send()

        @pl.when(jnp.logical_not(first))
        def _():
            leave(0, 0, jnp.int32(0)).wait_recv()
            entry(me).wait_send()
            for m in range(micro):
                for j in range(per):
                    back(m, j).wait_send()

        @pl.when(jnp.logical_not(last))
        def _():
            for m in range(micro):
                for c in range(chunks):
                    onward(m, c).wait_send()

        out[...] = share[...]

    vmem = pl.BlockSpec(memory_space=pltpu.VMEM)
    hbm = pl.BlockSpec(memory_space=pl.ANY)
    dma = pltpu.SemaphoreType.DMA
    block = (micro, rows, model)
    tall = embeds * rows
    return pl.pallas_call(
        body,
        in_specs=[vmem, hbm, vmem, vmem, vmem, hbm, hbm],
        out_specs=vmem,
        out_shape=jax.ShapeDtypeStruct((look, model), BF),
        scratch_shapes=[
            pltpu.VMEM(block, BF), pltpu.VMEM(block, BF), pltpu.VMEM(block, BF), pltpu.VMEM(block, BF),
            pltpu.VMEM((look, model), BF),
            pltpu.VMEM((model, inner), BF), pltpu.VMEM((inner, model), BF),
            pltpu.VMEM((inner, model), BF), pltpu.VMEM((model, inner), BF),
            pltpu.VMEM((micro, tall, width), F32), pltpu.VMEM((micro, rows, width), F32),
            pltpu.VMEM((micro, rows, inner), BF),
            pltpu.VMEM((tall, model), BF), pltpu.VMEM((rows, model), BF), pltpu.VMEM((rows, inner), BF),
            pltpu.VMEM((rows, model), F32), pltpu.VMEM((tall, width), BF), pltpu.VMEM((tall, model), F32),
            dma((2,)), dma((micro,)), dma((micro, chunks)), dma((micro, chunks)),
            dma((micro, per)), dma((micro, per)),
            dma, dma((stages,)), dma((stages,)), dma, dma,
        ],
        compiler_params=pltpu.CompilerParams(
            collective_id=0, has_side_effects=True, vmem_limit_bytes=60 << 20
        ),
        name="layer_pipeline",
    )(shares, top, mix, unmix, gain, w_up, w_down)


def mixers(proj):
    embeds, width = proj.shape
    mix = jnp.broadcast_to(proj[:, None, :], (embeds, width, width)).reshape(embeds * width, width)
    unmix = jnp.broadcast_to(proj.T[:, :, None], (width, embeds, width)).reshape(width, embeds * width)
    return mix, unmix


def per_device(
    emb_table,
    lcb_weight,
    fm_proj,
    norm_gain,
    w_up,
    w_down,
    top_grad,
    lookup_slot,
    wanted_rows,
    row_counts,
):
    section_count = lax.axis_size("section")
    owners = section_count * lax.axis_size("table")
    cap = wanted_rows.shape[2]
    rows_here, embed_width = emb_table.shape
    picked_rows = wanted_rows[0]


    def exchange(rows):
        rows = rows.reshape(owners, cap, embed_width)
        rows = lax.all_to_all(rows, ("section", "table"), split_axis=0, concat_axis=0, tiled=True)
        return rows.reshape(owners * cap, embed_width)

    fetched = exchange(gather_rows(emb_table, picked_rows.reshape(-1)))
    model_width = top_grad.shape[3]
    matrix = lookup_matrix(lookup_slot[0], lcb_weight, owners, cap)
    shares = compress(matrix, fetched, lcb_weight.shape[0])
    mix, unmix = mixers(fm_proj[0])
    lead_share = layer_pipeline(
        shares,
        top_grad.reshape(-1, model_width),
        mix,
        unmix,
        norm_gain.astype(F32),
        w_up[0],
        w_down[0],
        section_count,
        MICRO_ROWS,
    )
    returned = exchange(expand(matrix, lead_share, fetched, DECAY_WEIGHT))
    live_slots = jnp.arange(cap)[None, :] < row_counts[0][:, None]
    targets = jnp.where(live_slots, picked_rows, rows_here).reshape(-1)
    return scatter_rows(returned, targets, rows_here)


def solution(mesh):
    in_specs = (
        P(("section", "table"), None),
        P(),
        P("section", None, None),
        P("section", None),
        P("section", None, None),
        P("section", None, None),
        P("table", None, None, None),
        P("table", "section", None),
        P(("section", "table"), None, None),
        P(("section", "table"), None),
    )
    out_specs = P(("section", "table"), None)
    return jax.shard_map(
        per_device, mesh=mesh, in_specs=in_specs, out_specs=out_specs, check_vma=False
    )
```

```python
import jax
import jax.numpy as jnp
from jax import lax
from jax.experimental import pallas as pl
from jax.experimental.pallas import tpu as pltpu
from jax.sharding import PartitionSpec as P

BF = jnp.bfloat16
F32 = jnp.float32
NT = (((1,), (1,)), ((), ()))
TN = (((0,), (0,)), ((), ()))
EPSILON = 1e-05
DECAY_WEIGHT = 0.5
MICRO_ROWS = 128
CHUNK = 512


def scatter_rows(values, own, ids, rows, decay):
    count, width = values.shape
    block = 1024
    group = 16

    def body(idx, val, mine, out, acc, wide, sem):
        step = pl.program_id(0)

        @pl.when(step == 0)
        def _():
            acc[...] = jnp.zeros_like(acc)

        wide[...] = val[...].astype(F32) + decay * mine[...].astype(F32)

        @pl.loop(0, block // (4 * group))
        def _(part):
            for sub in range(4):
                at = part * (4 * group) + sub * group
                base = step * block + at
                where = [idx[base + j] for j in range(group)]
                new = [
                    acc[pl.ds(where[j], 1), :] + wide[pl.ds(at + j, 1), :]
                    for j in range(group)
                ]
                for j in range(group):
                    acc[pl.ds(where[j], 1), :] = new[j]

        @pl.when(step == pl.num_programs(0) - 1)
        def _():
            copy = pltpu.make_async_copy(acc.at[pl.ds(0, rows), :], out, sem)
            copy.start()
            copy.wait()

    return pl.pallas_call(
        body,
        grid=(count // block,),
        in_specs=[
            pl.BlockSpec(memory_space=pltpu.SMEM),
            pl.BlockSpec((block, width), lambda i: (i, 0)),
            pl.BlockSpec((block, width), lambda i: (i, 0)),
        ],
        out_specs=pl.BlockSpec(memory_space=pl.ANY),
        out_shape=jax.ShapeDtypeStruct((rows, width), F32),
        scratch_shapes=[
            pltpu.VMEM((rows + 8, width), F32),
            pltpu.VMEM((block, width), F32),
            pltpu.SemaphoreType.DMA,
        ],
        cost_estimate=pl.CostEstimate(flops=count * width, bytes_accessed=16 << 20, transcendentals=0),
        name="scatter_rows",
    )(ids, values, own)


def layer_forward(a_ref, mix, gain, w_up, w_down, keep, out_ref, last, ready, send):
    interact, inv_keep, hidden, prod, normed = keep
    rows, model = a_ref.shape
    width = mix.shape[1]
    embeds = model // width
    inner = w_up.shape[1]
    cols = [slice(k * width, (k + 1) * width) for k in range(embeds)]
    for k in range(embeds):
        for q in range(k, embeds):
            both = a_ref[:, cols[k]] * a_ref[:, cols[q]]
            prod[k * rows : (k + 1) * rows, cols[q]] = both
            if q > k:
                prod[q * rows : (q + 1) * rows, cols[k]] = both
    interact[...] = jnp.dot(prod[...], mix[...], preferred_element_type=F32)
    square = None
    for k in range(embeds):
        part = interact[k * rows : (k + 1) * rows, :]
        square = part * part if square is None else square + part * part
    inv = lax.rsqrt(jnp.sum(square, axis=1, keepdims=True) * (1.0 / model) + EPSILON)
    inv_keep[...] = jnp.broadcast_to(inv, (rows, width))
    for k in range(embeds):
        part = interact[k * rows : (k + 1) * rows, :]
        normed[:, cols[k]] = (part * inv * gain[:, cols[k]]).astype(BF)
    tile = min(512, inner)
    for n in range(0, inner, tile):
        before = jnp.dot(normed[...], w_up[:, n : n + tile], preferred_element_type=F32)
        hidden[:, n : n + tile] = jnp.maximum(before, 0.0).astype(BF)
    ready()

    @pl.when(jnp.logical_not(last))
    def _():
        tile = 256
        for n in range(0, model, tile):
            got = jnp.dot(hidden[...], w_down[:, n : n + tile], preferred_element_type=F32)
            out_ref[:, n : n + tile] = (got + a_ref[:, n : n + tile].astype(F32)).astype(BF)
            send(n, tile)


def layer_backward(a_ref, g_ref, unmix, gain, up_t, down_t, keep, gated, unit, pulled, spread, out_ref, send):
    interact, inv_keep, hidden, prod, normed = keep
    rows, model = a_ref.shape
    width = unmix.shape[0]
    embeds = model // width
    inner = down_t.shape[1]
    cols = [slice(k * width, (k + 1) * width) for k in range(embeds)]
    tile = min(512, inner)
    for n in range(0, inner, tile):
        up = jnp.dot(g_ref[...], down_t[:, n : n + tile], preferred_element_type=F32)
        gated[:, n : n + tile] = jnp.where(hidden[:, n : n + tile].astype(F32) > 0.0, up, 0.0).astype(BF)
    tile = 256
    cross = None
    for n in range(0, model, tile):
        got = jnp.dot(gated[...], up_t[:, n : n + tile], preferred_element_type=F32)
        got = got * gain[:, n : n + tile]
        unit[:, n : n + tile] = got
        for k in range(n // width, (n + tile) // width):
            part = got[:, k * width - n : (k + 1) * width - n] * interact[k * rows : (k + 1) * rows, :]
            cross = part if cross is None else cross + part
    mean = jnp.sum(cross, axis=1, keepdims=True) * (1.0 / model)
    inv = inv_keep[...]
    slope = inv * inv * mean
    for k in range(embeds):
        part = inv * (unit[:, cols[k]] - interact[k * rows : (k + 1) * rows, :] * slope)
        pulled[k * rows : (k + 1) * rows, :] = part.astype(BF)
    for q in range(0, embeds, 2):
        both = slice(q * width, (q + 2) * width)
        spread[:, both] = jnp.dot(pulled[...], unmix[:, both], preferred_element_type=F32)
    part_rows = 16
    for b in range(0, rows, part_rows):
        here = pl.ds(b, part_rows)
        a = [a_ref[here, cols[k]].astype(F32) for k in range(embeds)]
        total = [g_ref[here, cols[k]].astype(F32) for k in range(embeds)]
        for k in range(embeds):
            for q in range(k, embeds):
                pair = spread[pl.ds(k * rows + b, part_rows), cols[q]] + spread[pl.ds(q * rows + b, part_rows), cols[k]]
                total[k] = total[k] + pair * a[q]
                if q > k:
                    total[q] = total[q] + pair * a[k]
        for k in range(embeds):
            out_ref[here, cols[k]] = total[k].astype(BF)
        if (b + part_rows) % 32 == 0:
            send((b + part_rows) // 32 - 1)


def layer_pipeline(shares, top, mix, unmix, gain, w_up, w_down, stages, rows):
    look, model = shares.shape
    micro = top.shape[0] // rows
    per = rows // look
    inner = w_up.shape[1]
    width = mix.shape[1]
    embeds = model // width
    chunks = model // CHUNK
    copy_to = pltpu.make_async_remote_copy
    copy_here = pltpu.make_async_copy

    def body(
        share_in, top_in, mix_ref, unmix_ref, gain_ref, up_in, down_in, out,
        acts, cots, acts_out, cots_out, share, up_v, down_v, up_tv, down_tv,
        interact, inv_keep, hidden, prod, normed, gated, unit, pulled, spread,
        wsem, tsem, fsend, frecv, gsend, grecv, isend, irecv, osend, orecv, lsem,
    ):
        me = lax.axis_index("section")
        first, last = me == 0, me == stages - 1
        loads = [
            copy_here(src, dst, wsem.at[i])
            for i, (src, dst) in enumerate(
                [(up_in, up_v), (down_in, down_v)]
            )
        ]
        loads[0].start()
        loads[1].start()
        tops = [copy_here(top_in.at[pl.ds(m * rows, rows), :], cots.at[m], tsem.at[m]) for m in range(micro)]

        @pl.when(last)
        def _():
            for m in range(micro):
                tops[m].start()

        barrier = pltpu.get_barrier_semaphore()
        for d in range(1, stages):
            pl.semaphore_signal(
                barrier, inc=1, device_id={"section": lax.rem(me + d, stages)},
                device_id_type=pl.DeviceIdType.MESH,
            )
        pl.semaphore_wait(barrier, stages - 1)

        def entry(section):
            slot, off = section // per, lax.rem(section, per) * look
            return copy_to(
                src_ref=share_in, dst_ref=acts.at[slot, pl.ds(pl.multiple_of(off, look), look), :],
                send_sem=isend, recv_sem=irecv.at[section],
                device_id={"section": 0}, device_id_type=pl.DeviceIdType.MESH,
            )

        own = copy_here(share_in, acts.at[0, pl.ds(0, look), :], irecv.at[0])

        @pl.when(first)
        def _():
            own.start()
            own.wait()

        @pl.when(jnp.logical_not(first))
        def _():
            entry(me).start()

        def onward(m, c):
            piece = pl.ds(c * CHUNK, CHUNK)
            return copy_to(
                src_ref=acts_out.at[m, :, piece], dst_ref=acts.at[m, :, piece],
                send_sem=fsend.at[m, c], recv_sem=frecv.at[m, c],
                device_id={"section": lax.rem(me + 1, stages)}, device_id_type=pl.DeviceIdType.MESH,
            )

        def back(m, j):
            piece = pl.ds(j * look, look)
            return copy_to(
                src_ref=cots_out.at[m, piece, :], dst_ref=cots.at[m, piece, :],
                send_sem=gsend.at[m, j], recv_sem=grecv.at[m, j],
                device_id={"section": lax.rem(me + stages - 1, stages)}, device_id_type=pl.DeviceIdType.MESH,
            )

        def leave(m, j, section):
            return copy_to(
                src_ref=cots_out.at[m, pl.ds(j * look, look), :], dst_ref=share,
                send_sem=osend.at[section], recv_sem=orecv,
                device_id={"section": section}, device_id_type=pl.DeviceIdType.MESH,
            )

        keep_own = copy_here(cots_out.at[0, pl.ds(0, look), :], share, lsem)
        loads[0].wait()
        late = me > stages // 2

        def turn():
            tile = 256

            @pl.loop(0, inner // tile)
            def _(n):
                at = pl.ds(pl.multiple_of(n * tile, tile), tile)
                up_tv[at, :] = up_v[:, at].T
                down_tv[:, at] = down_v[at, :].T

        @pl.when(late)
        def _():
            loads[1].wait()
            turn()

        def step(i, carry):
            ahead = jnp.where(last, lax.rem(i, 2) == 0, i < micro)
            m = jnp.where(last, i // 2, lax.rem(i, micro))
            keep = (interact.at[m], inv_keep.at[m], hidden.at[m], prod, normed)

            @pl.when(ahead)
            def _():
                @pl.when(jnp.logical_not(first))
                def _():
                    for c in range(chunks):
                        onward(m, c).wait_recv()

                @pl.when(first)
                def _():
                    for j in range(per):
                        @pl.when(m * per + j > 0)
                        def _():
                            entry(m * per + j).wait_recv()

                def ready():
                    @pl.when((i == 0) & jnp.logical_not(late))
                    def _():
                        loads[1].wait()

                layer_forward(
                    acts.at[m], mix_ref, gain_ref, up_v, down_v, keep, acts_out.at[m], last, ready,
                    lambda n, tile: onward(m, n // CHUNK).start() if (n + tile) % CHUNK == 0 else None,
                )

            @pl.when(jnp.logical_not(ahead))
            def _():
                @pl.when((m == 0) & jnp.logical_not(late))
                def _():
                    turn()

                @pl.when(last)
                def _():
                    copy_here(top_in.at[pl.ds(pl.multiple_of(m * rows, rows), rows), :], cots.at[m], tsem.at[m]).wait()

                @pl.when(jnp.logical_not(last))
                def _():
                    for j in range(per):
                        back(m, j).wait_recv()

                def send(j):
                    @pl.when(jnp.logical_not(first))
                    def _():
                        back(m, j).start()

                    @pl.when(first)
                    def _():
                        section = m * per + j
                        if j == 0:
                            @pl.when(section == 0)
                            def _():
                                keep_own.start()

                            @pl.when(section > 0)
                            def _():
                                leave(m, j, section).start()
                        else:
                            leave(m, j, section).start()

                layer_backward(
                    acts.at[m], cots.at[m], unmix_ref, gain_ref, up_tv, down_tv, keep,
                    gated, unit, pulled, spread, cots_out.at[m], send,
                )

            return carry

        lax.fori_loop(0, 2 * micro, step, 0)

        @pl.when(first)
        def _():
            keep_own.wait()
            for section in range(1, stages):
                leave(section // per, section % per, jnp.int32(section)).wait_send()

        @pl.when(jnp.logical_not(first))
        def _():
            leave(0, 0, jnp.int32(0)).wait_recv()
            entry(me).wait_send()
            for m in range(micro):
                for j in range(per):
                    back(m, j).wait_send()

        @pl.when(jnp.logical_not(last))
        def _():
            for m in range(micro):
                for c in range(chunks):
                    onward(m, c).wait_send()

        out[...] = share[...]

    vmem = pl.BlockSpec(memory_space=pltpu.VMEM)
    hbm = pl.BlockSpec(memory_space=pl.ANY)
    dma = pltpu.SemaphoreType.DMA
    block = (micro, rows, model)
    tall = embeds * rows
    return pl.pallas_call(
        body,
        in_specs=[vmem, hbm, vmem, vmem, vmem, hbm, hbm],
        out_specs=vmem,
        out_shape=jax.ShapeDtypeStruct((look, model), BF),
        scratch_shapes=[
            pltpu.VMEM(block, BF), pltpu.VMEM(block, BF), pltpu.VMEM(block, BF), pltpu.VMEM(block, BF),
            pltpu.VMEM((look, model), BF),
            pltpu.VMEM((model, inner), BF), pltpu.VMEM((inner, model), BF),
            pltpu.VMEM((inner, model), BF), pltpu.VMEM((model, inner), BF),
            pltpu.VMEM((micro, tall, width), F32), pltpu.VMEM((micro, rows, width), F32),
            pltpu.VMEM((micro, rows, inner), BF),
            pltpu.VMEM((tall, model), BF), pltpu.VMEM((rows, model), BF), pltpu.VMEM((rows, inner), BF),
            pltpu.VMEM((rows, model), F32), pltpu.VMEM((tall, width), BF), pltpu.VMEM((tall, model), F32),
            dma((2,)), dma((micro,)), dma((micro, chunks)), dma((micro, chunks)),
            dma((micro, per)), dma((micro, per)),
            dma, dma((stages,)), dma((stages,)), dma, dma,
        ],
        compiler_params=pltpu.CompilerParams(
            collective_id=0, has_side_effects=True, vmem_limit_bytes=60 << 20
        ),
        name="layer_pipeline",
    )(shares, top, mix, unmix, gain, w_up, w_down)


def mixers(proj):
    embeds, width = proj.shape
    mix = jnp.broadcast_to(proj[:, None, :], (embeds, width, width)).reshape(embeds * width, width)
    unmix = jnp.broadcast_to(proj.T[:, :, None], (width, embeds, width)).reshape(width, embeds * width)
    return mix, unmix


def partner(j, tables):
    pairs = tables // 2
    order = lax.rem(j * 37, pairs * lax.axis_size("section"))
    return order // pairs, lax.rem(order, pairs)


def place(j, sign):
    sections, tables = lax.axis_size("section"), lax.axis_size("table")
    pairs = tables // 2
    step_s, step_t = partner(j, tables)
    section = lax.rem(lax.axis_index("section") + sections + sign * step_s, sections)
    pair = lax.rem(lax.axis_index("table") // 2 + pairs + sign * step_t, pairs)
    return section, pair


def greet(sections, tables):
    barrier = pltpu.get_barrier_semaphore()
    me_s, me_t = lax.axis_index("section"), lax.axis_index("table")

    def signal(d, carry):
        pl.semaphore_signal(
            barrier, inc=1,
            device_id=(lax.rem(me_s + d // tables, sections), lax.rem(me_t + lax.rem(d, tables), tables)),
            device_id_type=pl.DeviceIdType.MESH,
        )
        return carry

    lax.fori_loop(1, sections * tables, signal, 0)
    pl.semaphore_wait(barrier, sections * tables - 1)


def fetch_compress(table, ids, slots, lcb, cap):
    sections, tables = lax.axis_size("section"), lax.axis_size("table")
    owners = sections * tables
    pairs = owners // 2
    groups = 8
    rows, width = table.shape
    samples, features = slots.shape
    embeds = lcb.shape[0]
    shift = cap.bit_length() - 1

    def body(idx, tab, slot_ref, lcb_ref, sent_out, mat_out, shares, wide, tmp, stage, landed, mat, acc, ssem, rsem, lsem, osem):
        me_s, me_t = lax.axis_index("section"), lax.axis_index("table")
        me = me_s * tables + me_t
        wide[...] = tab[...].astype(F32)
        greet(sections, tables)

        def target(i):
            section, pair = place(i // 2, 1)
            return section, pair * 2 + lax.rem(me_t + lax.rem(i, 2), 2)

        def block(o):
            return pl.ds(pl.multiple_of(o * cap, cap), cap)

        def send(i):
            section, spot = target(i)
            return pltpu.make_async_remote_copy(
                src_ref=stage.at[block(section * tables + spot), :], dst_ref=landed.at[block(me), :],
                send_sem=ssem, recv_sem=rsem.at[i // (2 * pairs // groups)],
                device_id=(section, spot), device_id_type=pl.DeviceIdType.MESH,
            )

        own = pltpu.make_async_copy(stage.at[block(me), :], landed.at[block(me), :], lsem)

        def gather(i, carry):
            section, spot = target(i)
            base = (section * tables + spot) * cap
            for r in range(cap):
                tmp[pl.ds(r, 1), :] = wide[pl.ds(idx[base + r], 1), :]
            stage[pl.ds(pl.multiple_of(base, cap), cap), :] = tmp[...].astype(BF)

            @pl.when(i == 1)
            def _():
                own.start()

            @pl.when(i > 1)
            def _():
                send(i - 1).start()

            return carry

        lax.fori_loop(0, owners, gather, 0)
        send(owners - 1).start()
        keep = pltpu.make_async_copy(stage, sent_out, osem.at[0])
        keep.start()

        tiled = jnp.concatenate([lcb_ref[...].astype(F32)] * 2, axis=0).astype(BF)
        zero = jnp.zeros((), BF)
        lane = lax.broadcasted_iota(jnp.int32, (2 * cap, features), 0)
        row = (lax.broadcasted_iota(jnp.int32, (16, features), 0) // embeds).astype(F32).astype(BF)

        def select(p, carry):
            parts = []
            for h in range(2):
                slot = slot_ref[p, pl.ds(h, 1), :]
                pair = lax.shift_right_logical(slot, shift + 1)
                spot = slot & (2 * cap - 1)
                picks = jnp.where(lane == spot, 1.0, 0.0).astype(BF)
                pair16 = jnp.broadcast_to(pair.astype(F32), (16, features)).astype(BF)
                spread = jnp.concatenate(
                    [jnp.where(pair16 == row + jnp.asarray(float(o), BF), tiled, zero) for o in range(0, pairs, 2)],
                    axis=0,
                )
                got = lax.dot_general(spread, picks, NT, preferred_element_type=F32)
                parts.append(got.reshape(pairs, embeds, 2 * cap))
            mat[:, pl.ds(pl.multiple_of(p * 2 * embeds, 2 * embeds), 2 * embeds), :] = jnp.concatenate(parts, axis=1).astype(BF)
            return carry

        lax.fori_loop(0, samples // 2, select, 0)
        save = pltpu.make_async_copy(mat, mat_out, osem.at[1])
        save.start()
        acc[...] = jnp.zeros_like(acc)
        own.wait()

        def collect(g, carry):
            span = 2 * cap * (pairs // groups)

            @pl.when(g == 0)
            def _():
                part = pl.ds(0, span - cap)
                pltpu.make_async_copy(stage.at[part, :], landed.at[part, :], rsem.at[g]).wait()

            @pl.when(g > 0)
            def _():
                part = pl.ds(0, span)
                pltpu.make_async_copy(stage.at[part, :], landed.at[part, :], rsem.at[g]).wait()

            total = acc[...]
            for e in range(pairs // groups):
                section, pair = place(g * (pairs // groups) + e, -1)
                o = section * (tables // 2) + pair
                total += jnp.dot(
                    mat[o], landed[pl.ds(pl.multiple_of(o * 2 * cap, 2 * cap), 2 * cap), :],
                    preferred_element_type=F32,
                )
            acc[...] = total
            return carry

        lax.fori_loop(0, groups, collect, 0)
        for k in range(embeds):
            shares[:, k * width : (k + 1) * width] = acc[pl.ds(k, samples, stride=embeds), :].astype(BF)
        part = pl.ds(0, (owners - 1) * cap)
        pltpu.make_async_copy(stage.at[part, :], landed.at[part, :], ssem).wait()
        keep.wait()
        save.wait()

    vmem = pl.BlockSpec(memory_space=pltpu.VMEM)
    hbm = pl.BlockSpec(memory_space=pl.ANY)
    dma = pltpu.SemaphoreType.DMA
    return pl.pallas_call(
        body,
        in_specs=[pl.BlockSpec(memory_space=pltpu.SMEM), vmem, vmem, vmem],
        out_specs=[hbm, hbm, vmem],
        out_shape=[
            jax.ShapeDtypeStruct((owners * cap, width), BF),
            jax.ShapeDtypeStruct((pairs, samples * embeds, 2 * cap), BF),
            jax.ShapeDtypeStruct((samples, embeds * width), BF),
        ],
        scratch_shapes=[
            pltpu.VMEM((rows, width), F32), pltpu.VMEM((cap, width), F32),
            pltpu.VMEM((owners * cap, width), BF), pltpu.VMEM((owners * cap, width), BF),
            pltpu.VMEM((pairs, samples * embeds, 2 * cap), BF), pltpu.VMEM((samples * embeds, width), F32),
            dma, dma((groups,)), dma, dma((2,)),
        ],
        compiler_params=pltpu.CompilerParams(collective_id=1, has_side_effects=True, vmem_limit_bytes=60 << 20),
        name="fetch_compress",
    )(ids, table, slots.reshape(samples // 2, 2, features), lcb)


def expand_return(matrix, grads, cap):
    sections, tables = lax.axis_size("section"), lax.axis_size("table")
    owners = sections * tables
    pairs, outs, slots = matrix.shape
    samples, model = grads.shape
    embeds = outs // samples
    width = model // embeds
    groups = 8
    per = pairs // groups

    def body(mat_in, grad, landed, done, mat, wide, tall, stage, msem, ssem, rsem, lsem):
        me_s, me_t = lax.axis_index("section"), lax.axis_index("table")
        me = me_s * tables + me_t

        def load(j):
            section, pair = place(j, 1)
            o = section * (tables // 2) + pair
            return pltpu.make_async_copy(mat_in.at[o], mat.at[j], msem.at[j])

        def begin(j, carry):
            load(j).start()
            return carry

        lax.fori_loop(0, pairs, begin, 0)
        for k in range(embeds):
            wide[pl.ds(k, samples, stride=embeds), :] = grad[:, k * width : (k + 1) * width].astype(F32)
        tall[...] = wide[...].astype(BF)
        greet(sections, tables)

        def block(o):
            return pl.ds(pl.multiple_of(o * cap, cap), cap)

        def send(section, spot):
            return pltpu.make_async_remote_copy(
                src_ref=stage.at[block(section * tables + spot), :], dst_ref=landed.at[block(me), :],
                send_sem=ssem, recv_sem=rsem, device_id=(section, spot), device_id_type=pl.DeviceIdType.MESH,
            )

        own = pltpu.make_async_copy(stage.at[block(me), :], landed.at[block(me), :], lsem)

        def pair_out(j):
            section, pair = place(j, 1)

            @pl.when(j == 0)
            def _():
                own.start()
                send(me_s, me_t + 1 - 2 * lax.rem(me_t, 2)).start()

            @pl.when(j > 0)
            def _():
                for b in range(2):
                    send(section, pair * 2 + b).start()

        def work(j, carry):
            section, pair = place(j, 1)
            o = section * (tables // 2) + pair
            load(j).wait()
            got = lax.dot_general(mat[j], tall[...], TN, preferred_element_type=F32)
            stage[pl.ds(pl.multiple_of(o * slots, slots), slots), :] = got.astype(BF)

            @pl.when(j > 0)
            def _():
                pair_out(j - 1)

            return carry

        lax.fori_loop(0, pairs, work, 0)
        pair_out(jnp.int32(pairs - 1))
        own.wait()
        part = pl.ds(0, (owners - 1) * cap)
        pltpu.make_async_copy(stage.at[part, :], landed.at[part, :], rsem).wait()
        pltpu.make_async_copy(stage.at[part, :], landed.at[part, :], ssem).wait()
        done[...] = jnp.zeros_like(done)

    vmem = pl.BlockSpec(memory_space=pltpu.VMEM)
    hbm = pl.BlockSpec(memory_space=pl.ANY)
    dma = pltpu.SemaphoreType.DMA
    return pl.pallas_call(
        body,
        in_specs=[hbm, vmem],
        out_specs=[hbm, vmem],
        out_shape=[
            jax.ShapeDtypeStruct((owners * cap, width), BF),
            jax.ShapeDtypeStruct((8, 128), F32),
        ],
        scratch_shapes=[
            pltpu.VMEM(matrix.shape, BF), pltpu.VMEM((outs, width), F32), pltpu.VMEM((outs, width), BF),
            pltpu.VMEM((owners * cap, width), BF), dma((pairs,)), dma, dma, dma,
        ],
        compiler_params=pltpu.CompilerParams(collective_id=2, has_side_effects=True, vmem_limit_bytes=60 << 20),
        name="expand_return",
    )(matrix, grads)[0]


def per_device(
    emb_table,
    lcb_weight,
    fm_proj,
    norm_gain,
    w_up,
    w_down,
    top_grad,
    lookup_slot,
    wanted_rows,
    row_counts,
):
    section_count = lax.axis_size("section")
    cap = wanted_rows.shape[2]
    rows_here = emb_table.shape[0]
    picked_rows = wanted_rows[0]

    model_width = top_grad.shape[3]
    sent, matrix, shares = fetch_compress(
        emb_table, picked_rows.reshape(-1), lookup_slot[0], lcb_weight, cap
    )
    mix, unmix = mixers(fm_proj[0])
    lead_share = layer_pipeline(
        shares,
        top_grad.reshape(-1, model_width),
        mix,
        unmix,
        norm_gain.astype(F32),
        w_up[0],
        w_down[0],
        section_count,
        MICRO_ROWS,
    )
    returned = expand_return(matrix, lead_share, cap)
    live_slots = jnp.arange(cap)[None, :] < row_counts[0][:, None]
    targets = jnp.where(live_slots, picked_rows, rows_here).reshape(-1)
    return scatter_rows(returned, sent, targets, rows_here, DECAY_WEIGHT)


def solution(mesh):
    in_specs = (
        P(("section", "table"), None),
        P(),
        P("section", None, None),
        P("section", None),
        P("section", None, None),
        P("section", None, None),
        P("table", None, None, None),
        P("table", "section", None),
        P(("section", "table"), None, None),
        P(("section", "table"), None),
    )
    out_specs = P(("section", "table"), None)
    return jax.shard_map(
        per_device, mesh=mesh, in_specs=in_specs, out_specs=out_specs, check_vma=False
    )
```

```python
import jax
import jax.numpy as jnp
from jax import lax
from jax.experimental import pallas as pl
from jax.experimental.pallas import tpu as pltpu
from jax.sharding import PartitionSpec as P

BF = jnp.bfloat16
F32 = jnp.float32
NT = (((1,), (1,)), ((), ()))
TN = (((0,), (0,)), ((), ()))
EPSILON = 1e-05
DECAY_WEIGHT = 0.5
MICRO_ROWS = 128
CHUNK = 512
WAYS = 4
GROUP = 4


def scatter_rows(values, own, ids, rows, decay):
    count, width = values.shape
    block = 1024
    cap = 128
    group = GROUP

    def body(idx, val, mine, out, *scratch):
        sums, (wide, sem) = scratch[:WAYS], scratch[WAYS:]
        step = pl.program_id(0)

        @pl.when(step == 0)
        def _():
            for total in sums:
                total[...] = jnp.zeros_like(total)

        wide[...] = val[...].astype(F32) + decay * mine[...].astype(F32)

        @pl.loop(0, block // (WAYS * cap))
        def _(part):
            for at in range(0, cap, group):
                for h, total in enumerate(sums):
                    start = part * (WAYS * cap) + h * cap + at
                    base = step * block + start
                    where = [idx[base + j] for j in range(group)]
                    new = [
                        total[pl.ds(where[j], 1), :] + wide[pl.ds(start + j, 1), :]
                        for j in range(group)
                    ]
                    for j in range(group):
                        total[pl.ds(where[j], 1), :] = new[j]

        @pl.when(step == pl.num_programs(0) - 1)
        def _():
            tile = 512
            copies = []
            for n in range(0, rows, tile):
                whole = sums[0][n : n + tile, :]
                for total in sums[1:]:
                    whole += total[n : n + tile, :]
                sums[0][n : n + tile, :] = whole
                copies.append(pltpu.make_async_copy(sums[0].at[pl.ds(n, tile), :], out.at[pl.ds(n, tile), :], sem.at[n // tile]))
                copies[-1].start()
            for copy in copies:
                copy.wait()

    return pl.pallas_call(
        body,
        grid=(count // block,),
        in_specs=[
            pl.BlockSpec(memory_space=pltpu.SMEM),
            pl.BlockSpec((block, width), lambda i: (i, 0)),
            pl.BlockSpec((block, width), lambda i: (i, 0)),
        ],
        out_specs=pl.BlockSpec(memory_space=pl.ANY),
        out_shape=jax.ShapeDtypeStruct((rows, width), F32),
        scratch_shapes=[
            *[pltpu.VMEM((rows + 8, width), F32)] * WAYS,
            pltpu.VMEM((block, width), F32),
            pltpu.SemaphoreType.DMA((rows // 512,)),
        ],
        name="scatter_rows",
    )(ids, values, own)


def column(ref, k, width, rows=slice(None)):
    chunk = ref.shape[-1]
    at = (k * width) % chunk
    return ref[k * width // chunk, rows, at : at + width]


def layer_forward(a_ref, mix, gain, w_up, w_down, keep, out_ref, last, ready, send):
    interact, inv_keep, hidden, prod, normed = keep
    chunks, rows, chunk = a_ref.shape
    model = chunks * chunk
    width = mix.shape[1]
    embeds = model // width
    inner = w_up.shape[1]
    cols = [slice(k * width, (k + 1) * width) for k in range(embeds)]
    for k in range(embeds):
        for q in range(k, embeds):
            both = column(a_ref, k, width) * column(a_ref, q, width)
            prod[k * rows : (k + 1) * rows, cols[q]] = both
            if q > k:
                prod[q * rows : (q + 1) * rows, cols[k]] = both
    interact[...] = jnp.dot(prod[...], mix[...], preferred_element_type=F32)
    square = None
    for k in range(embeds):
        part = interact[k * rows : (k + 1) * rows, :]
        square = part * part if square is None else square + part * part
    inv = lax.rsqrt(jnp.sum(square, axis=1, keepdims=True) * (1.0 / model) + EPSILON)
    inv_keep[...] = jnp.broadcast_to(inv, (rows, width))
    for k in range(embeds):
        part = interact[k * rows : (k + 1) * rows, :]
        normed[:, cols[k]] = (part * inv * gain[:, cols[k]]).astype(BF)
    tile = min(512, inner)
    for n in range(0, inner, tile):
        before = jnp.dot(normed[...], w_up[:, n : n + tile], preferred_element_type=F32)
        hidden[:, n : n + tile] = jnp.maximum(before, 0.0).astype(BF)
    ready()

    @pl.when(jnp.logical_not(last))
    def _():
        for c in range(chunks):
            got = jnp.dot(hidden[...], w_down[:, c * chunk : (c + 1) * chunk], preferred_element_type=F32)
            out_ref[c] = (got + a_ref[c].astype(F32)).astype(BF)
            send(c)


def layer_backward(a_ref, g_ref, unmix, gain, up_t, down_t, keep, gated, unit, pulled, spread, out_ref, send):
    interact, inv_keep, hidden, prod, normed = keep
    rows, model = g_ref.shape
    width = unmix.shape[0]
    embeds = model // width
    inner = down_t.shape[1]
    cols = [slice(k * width, (k + 1) * width) for k in range(embeds)]
    tile = min(512, inner)
    for n in range(0, inner, tile):
        up = jnp.dot(g_ref[...], down_t[:, n : n + tile], preferred_element_type=F32)
        gated[:, n : n + tile] = jnp.where(hidden[:, n : n + tile].astype(F32) > 0.0, up, 0.0).astype(BF)
    tile = 256
    cross = None
    for n in range(0, model, tile):
        got = jnp.dot(gated[...], up_t[:, n : n + tile], preferred_element_type=F32)
        got = got * gain[:, n : n + tile]
        unit[:, n : n + tile] = got
        for k in range(n // width, (n + tile) // width):
            part = got[:, k * width - n : (k + 1) * width - n] * interact[k * rows : (k + 1) * rows, :]
            cross = part if cross is None else cross + part
    mean = jnp.sum(cross, axis=1, keepdims=True) * (1.0 / model)
    inv = inv_keep[...]
    slope = inv * inv * mean
    for k in range(embeds):
        part = inv * (unit[:, cols[k]] - interact[k * rows : (k + 1) * rows, :] * slope)
        pulled[k * rows : (k + 1) * rows, :] = part.astype(BF)
    for q in range(0, embeds, 2):
        both = slice(q * width, (q + 2) * width)
        spread[:, both] = jnp.dot(pulled[...], unmix[:, both], preferred_element_type=F32)
    part_rows = 16
    for b in range(0, rows, part_rows):
        here = pl.ds(b, part_rows)
        a = [column(a_ref, k, width, here).astype(F32) for k in range(embeds)]
        total = [g_ref[here, cols[k]].astype(F32) for k in range(embeds)]
        for k in range(embeds):
            for q in range(k, embeds):
                pair = spread[pl.ds(k * rows + b, part_rows), cols[q]] + spread[pl.ds(q * rows + b, part_rows), cols[k]]
                total[k] = total[k] + pair * a[q]
                if q > k:
                    total[q] = total[q] + pair * a[k]
        for k in range(embeds):
            out_ref[here, cols[k]] = total[k].astype(BF)
        if (b + part_rows) % 32 == 0:
            send((b + part_rows) // 32 - 1)


def layer_pipeline(shares, top, proj, gain, w_up, w_down, stages, rows):
    chunks, look, chunk = shares.shape
    model = chunks * chunk
    micro = top.shape[0] // rows
    per = rows // look
    inner = w_up.shape[1]
    embeds, width = proj.shape
    copy_to = pltpu.make_async_remote_copy
    copy_here = pltpu.make_async_copy

    def body(
        share_in, top_in, proj_ref, gain_in, up_in, down_in, out,
        acts, cots, acts_out, cots_out, share, up_v, down_v, up_tv, down_tv,
        interact, inv_keep, hidden, prod, normed, gated, unit, pulled, spread,
        mix_ref, unmix_ref, gain_ref,
        wsem, tsem, fsend, frecv, gsend, grecv, isend, irecv, osend, orecv, lsem,
    ):
        me = lax.axis_index("section")
        first, last = me == 0, me == stages - 1
        loads = [
            copy_here(src, dst, wsem.at[i])
            for i, (src, dst) in enumerate(
                [(up_in, up_v), (down_in, down_v)]
            )
        ]
        loads[0].start()
        tops = [copy_here(top_in.at[pl.ds(m * rows, rows), :], cots.at[m], tsem.at[m]) for m in range(micro)]

        @pl.when(last)
        def _():
            for m in range(micro):
                tops[m].start()

        gain_ref[...] = gain_in[...].astype(F32)
        narrow = proj_ref[...].astype(F32)
        for k in range(embeds):
            part = slice(k * width, (k + 1) * width)
            line = jnp.broadcast_to(narrow[k : k + 1, :], (width, width))
            mix_ref[part, :] = line.astype(BF)
            unmix_ref[:, part] = line.T.astype(BF)
        barrier = pltpu.get_barrier_semaphore()
        for d in range(1, stages):
            pl.semaphore_signal(
                barrier, inc=1, device_id={"section": lax.rem(me + d, stages)},
                device_id_type=pl.DeviceIdType.MESH,
            )
        pl.semaphore_wait(barrier, stages - 1)

        def entry(section):
            slot, off = section // per, lax.rem(section, per) * look
            return copy_to(
                src_ref=share_in, dst_ref=acts.at[slot, :, pl.ds(pl.multiple_of(off, look), look), :],
                send_sem=isend, recv_sem=irecv.at[section],
                device_id={"section": 0}, device_id_type=pl.DeviceIdType.MESH,
            )

        own = copy_here(share_in, acts.at[0, :, pl.ds(0, look), :], irecv.at[0])

        @pl.when(first)
        def _():
            own.start()
            own.wait()

        @pl.when(jnp.logical_not(first))
        def _():
            entry(me).start()

        def onward(m, c):
            return copy_to(
                src_ref=acts_out.at[m, c], dst_ref=acts.at[m, c],
                send_sem=fsend.at[m, c], recv_sem=frecv.at[m, c],
                device_id={"section": lax.rem(me + 1, stages)}, device_id_type=pl.DeviceIdType.MESH,
            )

        def back(m, j):
            piece = pl.ds(j * look, look)
            return copy_to(
                src_ref=cots_out.at[m, piece, :], dst_ref=cots.at[m, piece, :],
                send_sem=gsend.at[m, j], recv_sem=grecv.at[m, j],
                device_id={"section": lax.rem(me + stages - 1, stages)}, device_id_type=pl.DeviceIdType.MESH,
            )

        def leave(m, j, section):
            return copy_to(
                src_ref=cots_out.at[m, pl.ds(j * look, look), :], dst_ref=share,
                send_sem=osend.at[section], recv_sem=orecv,
                device_id={"section": section}, device_id_type=pl.DeviceIdType.MESH,
            )

        keep_own = copy_here(cots_out.at[0, pl.ds(0, look), :], share, lsem)
        loads[0].wait()
        loads[1].start()
        late = me > stages // 2

        def turn():
            tile = 256

            @pl.loop(0, inner // tile)
            def _(n):
                at = pl.ds(pl.multiple_of(n * tile, tile), tile)
                up_tv[at, :] = up_v[:, at].T
                down_tv[:, at] = down_v[at, :].T

        @pl.when(late)
        def _():
            loads[1].wait()
            turn()

        def step(i, carry):
            ahead = jnp.where(last, lax.rem(i, 2) == 0, i < micro)
            m = jnp.where(last, i // 2, lax.rem(i, micro))
            keep = (interact.at[m], inv_keep.at[m], hidden.at[m], prod, normed)

            @pl.when(ahead)
            def _():
                @pl.when(jnp.logical_not(first))
                def _():
                    for c in range(chunks):
                        onward(m, c).wait_recv()

                @pl.when(first)
                def _():
                    for j in range(per):
                        @pl.when(m * per + j > 0)
                        def _():
                            entry(m * per + j).wait_recv()

                def ready():
                    @pl.when((i == 0) & jnp.logical_not(late))
                    def _():
                        loads[1].wait()

                layer_forward(
                    acts.at[m], mix_ref, gain_ref, up_v, down_v, keep, acts_out.at[m], last, ready,
                    lambda c: onward(m, c).start(),
                )

            @pl.when(jnp.logical_not(ahead))
            def _():
                @pl.when((m == 0) & jnp.logical_not(late))
                def _():
                    turn()

                @pl.when(last)
                def _():
                    copy_here(top_in.at[pl.ds(pl.multiple_of(m * rows, rows), rows), :], cots.at[m], tsem.at[m]).wait()

                @pl.when(jnp.logical_not(last))
                def _():
                    for j in range(per):
                        back(m, j).wait_recv()

                def send(j):
                    @pl.when(jnp.logical_not(first))
                    def _():
                        back(m, j).start()

                    @pl.when(first)
                    def _():
                        section = m * per + j
                        if j == 0:
                            @pl.when(section == 0)
                            def _():
                                keep_own.start()

                            @pl.when(section > 0)
                            def _():
                                leave(m, j, section).start()
                        else:
                            leave(m, j, section).start()

                layer_backward(
                    acts.at[m], cots.at[m], unmix_ref, gain_ref, up_tv, down_tv, keep,
                    gated, unit, pulled, spread, cots_out.at[m], send,
                )

            return carry

        lax.fori_loop(0, 2 * micro, step, 0)

        @pl.when(first)
        def _():
            keep_own.wait()
            for section in range(1, stages):
                leave(section // per, section % per, jnp.int32(section)).wait_send()

        @pl.when(jnp.logical_not(first))
        def _():
            leave(0, 0, jnp.int32(0)).wait_recv()
            entry(me).wait_send()
            for m in range(micro):
                for j in range(per):
                    back(m, j).wait_send()

        @pl.when(jnp.logical_not(last))
        def _():
            for m in range(micro):
                for c in range(chunks):
                    onward(m, c).wait_send()

        out[...] = share[...]

    vmem = pl.BlockSpec(memory_space=pltpu.VMEM)
    hbm = pl.BlockSpec(memory_space=pl.ANY)
    dma = pltpu.SemaphoreType.DMA
    block = (micro, rows, model)
    wide = (micro, chunks, rows, chunk)
    tall = embeds * rows
    return pl.pallas_call(
        body,
        in_specs=[vmem, hbm, vmem, vmem, hbm, hbm],
        out_specs=vmem,
        out_shape=jax.ShapeDtypeStruct((look, model), BF),
        scratch_shapes=[
            pltpu.VMEM(wide, BF), pltpu.VMEM(block, BF), pltpu.VMEM(wide, BF), pltpu.VMEM(block, BF),
            pltpu.VMEM((look, model), BF),
            pltpu.VMEM((model, inner), BF), pltpu.VMEM((inner, model), BF),
            pltpu.VMEM((inner, model), BF), pltpu.VMEM((model, inner), BF),
            pltpu.VMEM((micro, tall, width), F32), pltpu.VMEM((micro, rows, width), F32),
            pltpu.VMEM((micro, rows, inner), BF),
            pltpu.VMEM((tall, model), BF), pltpu.VMEM((rows, model), BF), pltpu.VMEM((rows, inner), BF),
            pltpu.VMEM((rows, model), F32), pltpu.VMEM((tall, width), BF), pltpu.VMEM((tall, model), F32),
            pltpu.VMEM((model, width), BF), pltpu.VMEM((width, model), BF), pltpu.VMEM((1, model), F32),
            dma((2,)), dma((micro,)), dma((micro, chunks)), dma((micro, chunks)),
            dma((micro, per)), dma((micro, per)),
            dma, dma((stages,)), dma((stages,)), dma, dma,
        ],
        compiler_params=pltpu.CompilerParams(
            collective_id=0, has_side_effects=True, vmem_limit_bytes=60 << 20
        ),
        name="layer_pipeline",
    )(shares, top, proj, gain, w_up, w_down)


def partner(j, tables):
    pairs = tables // 2
    order = lax.rem(j * 37, pairs * lax.axis_size("section"))
    return order // pairs, lax.rem(order, pairs)


def place(j, sign):
    sections, tables = lax.axis_size("section"), lax.axis_size("table")
    pairs = tables // 2
    step_s, step_t = partner(j, tables)
    section = lax.rem(lax.axis_index("section") + sections + sign * step_s, sections)
    pair = lax.rem(lax.axis_index("table") // 2 + pairs + sign * step_t, pairs)
    return section, pair


def greet(sections, tables):
    barrier = pltpu.get_barrier_semaphore()
    me_s, me_t = lax.axis_index("section"), lax.axis_index("table")

    def signal(d, carry):
        pl.semaphore_signal(
            barrier, inc=1,
            device_id=(lax.rem(me_s + d // tables, sections), lax.rem(me_t + lax.rem(d, tables), tables)),
            device_id_type=pl.DeviceIdType.MESH,
        )
        return carry

    lax.fori_loop(1, sections * tables, signal, 0)
    pl.semaphore_wait(barrier, sections * tables - 1)


def fetch_compress(table, wanted, counts, slots, lcb, chunk):
    sections, tables = lax.axis_size("section"), lax.axis_size("table")
    owners = sections * tables
    pairs = owners // 2
    groups = 8
    rows, width = table.shape
    samples, features = slots.shape
    cap = wanted.shape[1]
    embeds = lcb.shape[0]
    shift = cap.bit_length() - 1

    def body(idx, tab, wanted_ref, count_ref, slot_ref, lcb_ref, sent_out, mat_out, targets, shares, wide, tmp, stage, landed, mat, acc, ssem, rsem, lsem, osem):
        me_s, me_t = lax.axis_index("section"), lax.axis_index("table")
        me = me_s * tables + me_t
        wide[...] = tab[...].astype(F32)
        greet(sections, tables)

        def target(i):
            section, pair = place(i // 2, 1)
            return section, pair * 2 + lax.rem(me_t + lax.rem(i, 2), 2)

        def block(o):
            return pl.ds(pl.multiple_of(o * cap, cap), cap)

        def send(i):
            section, spot = target(i)
            return pltpu.make_async_remote_copy(
                src_ref=stage.at[block(section * tables + spot), :], dst_ref=landed.at[block(me), :],
                send_sem=ssem, recv_sem=rsem.at[i // (2 * pairs // groups)],
                device_id=(section, spot), device_id_type=pl.DeviceIdType.MESH,
            )

        own = pltpu.make_async_copy(stage.at[block(me), :], landed.at[block(me), :], lsem)

        def gather(i, carry):
            section, spot = target(i)
            base = (section * tables + spot) * cap
            for r in range(cap):
                tmp[pl.ds(r, 1), :] = wide[pl.ds(idx[base + r], 1), :]
            stage[pl.ds(pl.multiple_of(base, cap), cap), :] = tmp[...].astype(BF)

            @pl.when(i == 1)
            def _():
                own.start()

            @pl.when(i > 1)
            def _():
                send(i - 1).start()

            return carry

        lax.fori_loop(0, owners, gather, 0)
        send(owners - 1).start()
        keep = pltpu.make_async_copy(stage, sent_out, osem.at[0])
        keep.start()

        tiled = jnp.concatenate([lcb_ref[...].astype(F32)] * 2, axis=0).astype(BF)
        zero = jnp.zeros((), BF)
        lane = lax.broadcasted_iota(jnp.int32, (2 * cap, features), 0)
        row = (lax.broadcasted_iota(jnp.int32, (16, features), 0) // embeds).astype(F32).astype(BF)

        def select(p, carry):
            parts = []
            for h in range(2):
                slot = slot_ref[pl.ds(p * 2 + h, 1), :]
                pair = lax.shift_right_logical(slot, shift + 1)
                spot = slot & (2 * cap - 1)
                picks = jnp.where(lane == spot, 1.0, 0.0).astype(BF)
                pair16 = jnp.broadcast_to(pair.astype(F32), (16, features)).astype(BF)
                spread = jnp.concatenate(
                    [jnp.where(pair16 == row + jnp.asarray(float(o), BF), tiled, zero) for o in range(0, pairs, 2)],
                    axis=0,
                )
                got = lax.dot_general(spread, picks, NT, preferred_element_type=F32)
                parts.append(got.reshape(pairs, embeds, 2 * cap))
            mat[:, pl.ds(pl.multiple_of(p * 2 * embeds, 2 * embeds), 2 * embeds), :] = jnp.concatenate(parts, axis=1).astype(BF)
            return carry

        lax.fori_loop(0, samples // 2, select, 0)
        save = pltpu.make_async_copy(mat, mat_out, osem.at[1])
        save.start()
        live = jnp.broadcast_to(count_ref[...].astype(F32), (owners, owners)).T
        spot = lax.broadcasted_iota(jnp.int32, (owners, cap), 1).astype(F32)
        targets[...] = jnp.where(spot < live[:, :cap], wanted_ref[...], rows)
        acc[...] = jnp.zeros_like(acc)
        own.wait()

        def collect(g, carry):
            span = 2 * cap * (pairs // groups)

            @pl.when(g == 0)
            def _():
                part = pl.ds(0, span - cap)
                pltpu.make_async_copy(stage.at[part, :], landed.at[part, :], rsem.at[g]).wait()

            @pl.when(g > 0)
            def _():
                part = pl.ds(0, span)
                pltpu.make_async_copy(stage.at[part, :], landed.at[part, :], rsem.at[g]).wait()

            total = acc[...]
            for e in range(pairs // groups):
                section, pair = place(g * (pairs // groups) + e, -1)
                o = section * (tables // 2) + pair
                total += jnp.dot(
                    mat[o], landed[pl.ds(pl.multiple_of(o * 2 * cap, 2 * cap), 2 * cap), :],
                    preferred_element_type=F32,
                )
            acc[...] = total
            return carry

        lax.fori_loop(0, groups, collect, 0)
        for k in range(embeds):
            at = (k * width) % chunk
            shares[k * width // chunk, :, at : at + width] = acc[pl.ds(k, samples, stride=embeds), :].astype(BF)
        part = pl.ds(0, (owners - 1) * cap)
        pltpu.make_async_copy(stage.at[part, :], landed.at[part, :], ssem).wait()
        keep.wait()
        save.wait()

    vmem = pl.BlockSpec(memory_space=pltpu.VMEM)
    hbm = pl.BlockSpec(memory_space=pl.ANY)
    dma = pltpu.SemaphoreType.DMA
    return pl.pallas_call(
        body,
        in_specs=[pl.BlockSpec(memory_space=pltpu.SMEM), vmem, vmem, vmem, vmem, vmem],
        out_specs=[hbm, hbm, vmem, vmem],
        out_shape=[
            jax.ShapeDtypeStruct((owners * cap, width), BF),
            jax.ShapeDtypeStruct((pairs, samples * embeds, 2 * cap), BF),
            jax.ShapeDtypeStruct((owners, cap), jnp.int32),
            jax.ShapeDtypeStruct((embeds * width // chunk, samples, chunk), BF),
        ],
        scratch_shapes=[
            pltpu.VMEM((rows, width), F32), pltpu.VMEM((cap, width), F32),
            pltpu.VMEM((owners * cap, width), BF), pltpu.VMEM((owners * cap, width), BF),
            pltpu.VMEM((pairs, samples * embeds, 2 * cap), BF), pltpu.VMEM((samples * embeds, width), F32),
            dma, dma((groups,)), dma, dma((2,)),
        ],
        compiler_params=pltpu.CompilerParams(collective_id=1, has_side_effects=True, vmem_limit_bytes=60 << 20),
        name="fetch_compress",
    )(wanted.reshape(-1), table, wanted, counts, slots, lcb)


def expand_return(matrix, grads, cap):
    sections, tables = lax.axis_size("section"), lax.axis_size("table")
    owners = sections * tables
    pairs, outs, slots = matrix.shape
    samples, model = grads.shape
    embeds = outs // samples
    width = model // embeds
    groups = 8
    per = pairs // groups

    def body(mat_in, grad, landed, done, mat, wide, tall, stage, msem, ssem, rsem, lsem):
        me_s, me_t = lax.axis_index("section"), lax.axis_index("table")
        me = me_s * tables + me_t

        def load(j):
            section, pair = place(j, 1)
            o = section * (tables // 2) + pair
            return pltpu.make_async_copy(mat_in.at[o], mat.at[j], msem.at[j])

        def begin(j, carry):
            load(j).start()
            return carry

        lax.fori_loop(0, pairs, begin, 0)
        for k in range(embeds):
            wide[pl.ds(k, samples, stride=embeds), :] = grad[:, k * width : (k + 1) * width].astype(F32)
        tall[...] = wide[...].astype(BF)
        greet(sections, tables)

        def block(o):
            return pl.ds(pl.multiple_of(o * cap, cap), cap)

        def send(section, spot):
            return pltpu.make_async_remote_copy(
                src_ref=stage.at[block(section * tables + spot), :], dst_ref=landed.at[block(me), :],
                send_sem=ssem, recv_sem=rsem, device_id=(section, spot), device_id_type=pl.DeviceIdType.MESH,
            )

        own = pltpu.make_async_copy(stage.at[block(me), :], landed.at[block(me), :], lsem)

        def pair_out(j):
            section, pair = place(j, 1)

            @pl.when(j == 0)
            def _():
                own.start()
                send(me_s, me_t + 1 - 2 * lax.rem(me_t, 2)).start()

            @pl.when(j > 0)
            def _():
                for b in range(2):
                    send(section, pair * 2 + b).start()

        def work(j, carry):
            section, pair = place(j, 1)
            o = section * (tables // 2) + pair
            load(j).wait()
            got = lax.dot_general(mat[j], tall[...], TN, preferred_element_type=F32)
            stage[pl.ds(pl.multiple_of(o * slots, slots), slots), :] = got.astype(BF)

            @pl.when(j > 0)
            def _():
                pair_out(j - 1)

            return carry

        lax.fori_loop(0, pairs, work, 0)
        pair_out(jnp.int32(pairs - 1))
        own.wait()
        part = pl.ds(0, (owners - 1) * cap)
        pltpu.make_async_copy(stage.at[part, :], landed.at[part, :], rsem).wait()
        pltpu.make_async_copy(stage.at[part, :], landed.at[part, :], ssem).wait()
        done[...] = jnp.zeros_like(done)

    vmem = pl.BlockSpec(memory_space=pltpu.VMEM)
    hbm = pl.BlockSpec(memory_space=pl.ANY)
    dma = pltpu.SemaphoreType.DMA
    return pl.pallas_call(
        body,
        in_specs=[hbm, vmem],
        out_specs=[hbm, vmem],
        out_shape=[
            jax.ShapeDtypeStruct((owners * cap, width), BF),
            jax.ShapeDtypeStruct((8, 128), F32),
        ],
        scratch_shapes=[
            pltpu.VMEM(matrix.shape, BF), pltpu.VMEM((outs, width), F32), pltpu.VMEM((outs, width), BF),
            pltpu.VMEM((owners * cap, width), BF), dma((pairs,)), dma, dma, dma,
        ],
        compiler_params=pltpu.CompilerParams(collective_id=2, has_side_effects=True, vmem_limit_bytes=60 << 20),
        name="expand_return",
    )(matrix, grads)[0]


def per_device(
    emb_table,
    lcb_weight,
    fm_proj,
    norm_gain,
    w_up,
    w_down,
    top_grad,
    lookup_slot,
    wanted_rows,
    row_counts,
):
    section_count = lax.axis_size("section")
    cap = wanted_rows.shape[2]

    model_width = top_grad.shape[3]
    sent, matrix, targets, shares = fetch_compress(
        emb_table, wanted_rows[0], row_counts, lookup_slot[0], lcb_weight, CHUNK
    )
    lead_share = layer_pipeline(
        shares,
        top_grad.reshape(-1, model_width),
        fm_proj[0],
        norm_gain,
        w_up[0],
        w_down[0],
        section_count,
        MICRO_ROWS,
    )
    returned = expand_return(matrix, lead_share, cap)
    return scatter_rows(returned, sent, targets.reshape(-1), emb_table.shape[0], DECAY_WEIGHT)


def solution(mesh):
    in_specs = (
        P(("section", "table"), None),
        P(),
        P("section", None, None),
        P("section", None),
        P("section", None, None),
        P("section", None, None),
        P("table", None, None, None),
        P("table", "section", None),
        P(("section", "table"), None, None),
        P(("section", "table"), None),
    )
    out_specs = P(("section", "table"), None)
    return jax.shard_map(
        per_device, mesh=mesh, in_specs=in_specs, out_specs=out_specs, check_vma=False
    )
```

```python
import jax
import jax.numpy as jnp
from jax import lax
from jax.experimental import pallas as pl
from jax.experimental.pallas import tpu as pltpu
from jax.sharding import PartitionSpec as P

BF = jnp.bfloat16
F32 = jnp.float32
NT = (((1,), (1,)), ((), ()))
TN = (((0,), (0,)), ((), ()))
EPSILON = 1e-05
DECAY_WEIGHT = 0.5
MICRO_ROWS = 128
CHUNK = 512
WAYS = 4
GROUP = 4


def scatter_rows(values, own, ids, rows, decay):
    count, width = values.shape
    block = 1024
    cap = 128
    group = GROUP

    def body(idx, val, mine, out, *scratch):
        sums, (wide, sem) = scratch[:WAYS], scratch[WAYS:]
        step = pl.program_id(0)

        @pl.when(step == 0)
        def _():
            for total in sums:
                total[...] = jnp.zeros_like(total)

        wide[...] = val[...].astype(F32) + decay * mine[...].astype(F32)

        @pl.loop(0, block // (WAYS * cap))
        def _(part):
            for at in range(0, cap, group):
                for h, total in enumerate(sums):
                    start = part * (WAYS * cap) + h * cap + at
                    base = step * block + start
                    where = [idx[base + j] for j in range(group)]
                    new = [
                        total[pl.ds(where[j], 1), :] + wide[pl.ds(start + j, 1), :]
                        for j in range(group)
                    ]
                    for j in range(group):
                        total[pl.ds(where[j], 1), :] = new[j]

        @pl.when(step == pl.num_programs(0) - 1)
        def _():
            tile = 512
            copies = []
            for n in range(0, rows, tile):
                whole = sums[0][n : n + tile, :]
                for total in sums[1:]:
                    whole += total[n : n + tile, :]
                sums[0][n : n + tile, :] = whole
                copies.append(pltpu.make_async_copy(sums[0].at[pl.ds(n, tile), :], out.at[pl.ds(n, tile), :], sem.at[n // tile]))
                copies[-1].start()
            for copy in copies:
                copy.wait()

    return pl.pallas_call(
        body,
        grid=(count // block,),
        in_specs=[
            pl.BlockSpec(memory_space=pltpu.SMEM),
            pl.BlockSpec((block, width), lambda i: (i, 0)),
            pl.BlockSpec((block, width), lambda i: (i, 0)),
        ],
        out_specs=pl.BlockSpec(memory_space=pl.ANY),
        out_shape=jax.ShapeDtypeStruct((rows, width), F32),
        scratch_shapes=[
            *[pltpu.VMEM((rows + 8, width), F32)] * WAYS,
            pltpu.VMEM((block, width), F32),
            pltpu.SemaphoreType.DMA((rows // 512,)),
        ],
        name="scatter_rows",
    )(ids, values, own)


def column(ref, k, width, rows=slice(None)):
    chunk = ref.shape[-1]
    at = (k * width) % chunk
    return ref[k * width // chunk, rows, at : at + width]


def layer_forward(a_ref, mix, gain, w_up, w_down, keep, out_ref, last, ready, send):
    interact, inv_keep, hidden, prod, normed = keep
    chunks, rows, chunk = a_ref.shape
    model = chunks * chunk
    width = mix.shape[1]
    embeds = model // width
    inner = w_up.shape[1]
    cols = [slice(k * width, (k + 1) * width) for k in range(embeds)]
    for k in range(embeds):
        for q in range(k, embeds):
            both = column(a_ref, k, width) * column(a_ref, q, width)
            prod[k * rows : (k + 1) * rows, cols[q]] = both
            if q > k:
                prod[q * rows : (q + 1) * rows, cols[k]] = both
    interact[...] = jnp.dot(prod[...], mix[...], preferred_element_type=F32)
    square = None
    for k in range(embeds):
        part = interact[k * rows : (k + 1) * rows, :]
        square = part * part if square is None else square + part * part
    inv = lax.rsqrt(jnp.sum(square, axis=1, keepdims=True) * (1.0 / model) + EPSILON)
    inv_keep[...] = jnp.broadcast_to(inv, (rows, width))
    for k in range(embeds):
        part = interact[k * rows : (k + 1) * rows, :]
        normed[:, cols[k]] = (part * inv * gain[:, cols[k]]).astype(BF)
    tile = min(512, inner)
    for n in range(0, inner, tile):
        before = jnp.dot(normed[...], w_up[:, n : n + tile], preferred_element_type=F32)
        hidden[:, n : n + tile] = jnp.maximum(before, 0.0).astype(BF)
    ready()

    @pl.when(jnp.logical_not(last))
    def _():
        for c in range(chunks):
            got = jnp.dot(hidden[...], w_down[:, c * chunk : (c + 1) * chunk], preferred_element_type=F32)
            out_ref[c] = (got + a_ref[c].astype(F32)).astype(BF)
            send(c)


def layer_backward(a_ref, g_ref, unmix, gain, up_t, down_t, keep, gated, unit, pulled, spread, out_ref, send):
    interact, inv_keep, hidden, prod, normed = keep
    rows, model = g_ref.shape
    width = unmix.shape[0]
    embeds = model // width
    inner = down_t.shape[1]
    cols = [slice(k * width, (k + 1) * width) for k in range(embeds)]
    tile = min(512, inner)
    for n in range(0, inner, tile):
        up = jnp.dot(g_ref[...], down_t[:, n : n + tile], preferred_element_type=F32)
        gated[:, n : n + tile] = jnp.where(hidden[:, n : n + tile].astype(F32) > 0.0, up, 0.0).astype(BF)
    tile = 256
    cross = None
    for n in range(0, model, tile):
        got = jnp.dot(gated[...], up_t[:, n : n + tile], preferred_element_type=F32)
        got = got * gain[:, n : n + tile]
        unit[:, n : n + tile] = got
        for k in range(n // width, (n + tile) // width):
            part = got[:, k * width - n : (k + 1) * width - n] * interact[k * rows : (k + 1) * rows, :]
            cross = part if cross is None else cross + part
    mean = jnp.sum(cross, axis=1, keepdims=True) * (1.0 / model)
    inv = inv_keep[...]
    slope = inv * inv * mean
    for k in range(embeds):
        part = inv * (unit[:, cols[k]] - interact[k * rows : (k + 1) * rows, :] * slope)
        pulled[k * rows : (k + 1) * rows, :] = part.astype(BF)
    for q in range(0, embeds, 2):
        both = slice(q * width, (q + 2) * width)
        spread[:, both] = jnp.dot(pulled[...], unmix[:, both], preferred_element_type=F32)
    part_rows = 16
    for b in range(0, rows, part_rows):
        here = pl.ds(b, part_rows)
        a = [column(a_ref, k, width, here).astype(F32) for k in range(embeds)]
        total = [g_ref[here, cols[k]].astype(F32) for k in range(embeds)]
        for k in range(embeds):
            for q in range(k, embeds):
                pair = spread[pl.ds(k * rows + b, part_rows), cols[q]] + spread[pl.ds(q * rows + b, part_rows), cols[k]]
                total[k] = total[k] + pair * a[q]
                if q > k:
                    total[q] = total[q] + pair * a[k]
        for k in range(embeds):
            out_ref[here, cols[k]] = total[k].astype(BF)
        if (b + part_rows) % 32 == 0:
            send((b + part_rows) // 32 - 1)


def layer_pipeline(shares, top, proj, gain, w_up, w_down, stages, rows):
    chunks, look, chunk = shares.shape
    model = chunks * chunk
    micro = top.shape[0] // rows
    per = rows // look
    inner = w_up.shape[1]
    embeds, width = proj.shape
    copy_to = pltpu.make_async_remote_copy
    copy_here = pltpu.make_async_copy

    def body(
        share_in, top_in, proj_ref, gain_in, up_in, down_in, out,
        acts, cots, acts_out, cots_out, share, up_v, down_v, up_tv, down_tv,
        interact, inv_keep, hidden, prod, normed, gated, unit, pulled, spread,
        mix_ref, unmix_ref, gain_ref,
        wsem, tsem, fsend, frecv, gsend, grecv, isend, irecv, osend, orecv, lsem,
    ):
        me = lax.axis_index("section")
        first, last = me == 0, me == stages - 1
        loads = [
            copy_here(src, dst, wsem.at[i])
            for i, (src, dst) in enumerate(
                [(up_in, up_v), (down_in, down_v)]
            )
        ]
        loads[0].start()
        tops = [copy_here(top_in.at[pl.ds(m * rows, rows), :], cots.at[m], tsem.at[m]) for m in range(micro)]

        @pl.when(last)
        def _():
            for m in range(micro):
                tops[m].start()

        gain_ref[...] = gain_in[...].astype(F32)
        narrow = proj_ref[...].astype(F32)
        for k in range(embeds):
            part = slice(k * width, (k + 1) * width)
            line = jnp.broadcast_to(narrow[k : k + 1, :], (width, width))
            mix_ref[part, :] = line.astype(BF)
            unmix_ref[:, part] = line.T.astype(BF)
        barrier = pltpu.get_barrier_semaphore()
        for d in range(1, stages):
            pl.semaphore_signal(
                barrier, inc=1, device_id={"section": lax.rem(me + d, stages)},
                device_id_type=pl.DeviceIdType.MESH,
            )
        pl.semaphore_wait(barrier, stages - 1)

        def entry(section):
            slot, off = section // per, lax.rem(section, per) * look
            return copy_to(
                src_ref=share_in, dst_ref=acts.at[slot, :, pl.ds(pl.multiple_of(off, look), look), :],
                send_sem=isend, recv_sem=irecv.at[section],
                device_id={"section": 0}, device_id_type=pl.DeviceIdType.MESH,
            )

        own = copy_here(share_in, acts.at[0, :, pl.ds(0, look), :], irecv.at[0])

        @pl.when(first)
        def _():
            own.start()
            own.wait()

        @pl.when(jnp.logical_not(first))
        def _():
            entry(me).start()

        def onward(m, c):
            return copy_to(
                src_ref=acts_out.at[m, c], dst_ref=acts.at[m, c],
                send_sem=fsend.at[m, c], recv_sem=frecv.at[m, c],
                device_id={"section": lax.rem(me + 1, stages)}, device_id_type=pl.DeviceIdType.MESH,
            )

        def back(m, j):
            piece = pl.ds(j * look, look)
            return copy_to(
                src_ref=cots_out.at[m, piece, :], dst_ref=cots.at[m, piece, :],
                send_sem=gsend.at[m, j], recv_sem=grecv.at[m, j],
                device_id={"section": lax.rem(me + stages - 1, stages)}, device_id_type=pl.DeviceIdType.MESH,
            )

        def leave(m, j, section):
            return copy_to(
                src_ref=cots_out.at[m, pl.ds(j * look, look), :], dst_ref=share,
                send_sem=osend.at[section], recv_sem=orecv,
                device_id={"section": section}, device_id_type=pl.DeviceIdType.MESH,
            )

        keep_own = copy_here(cots_out.at[0, pl.ds(0, look), :], share, lsem)
        loads[0].wait()
        loads[1].start()
        late = me > stages // 2

        def turn():
            tile = 256

            @pl.loop(0, inner // tile)
            def _(n):
                at = pl.ds(pl.multiple_of(n * tile, tile), tile)
                up_tv[at, :] = up_v[:, at].T
                down_tv[:, at] = down_v[at, :].T

        @pl.when(late)
        def _():
            loads[1].wait()
            turn()

        def step(i, carry):
            ahead = jnp.where(last, lax.rem(i, 2) == 0, i < micro)
            m = jnp.where(last, i // 2, lax.rem(i, micro))
            keep = (interact.at[m], inv_keep.at[m], hidden.at[m], prod, normed)

            @pl.when(ahead)
            def _():
                @pl.when(jnp.logical_not(first))
                def _():
                    for c in range(chunks):
                        onward(m, c).wait_recv()

                @pl.when(first)
                def _():
                    for j in range(per):
                        @pl.when(m * per + j > 0)
                        def _():
                            entry(m * per + j).wait_recv()

                def ready():
                    @pl.when((i == 0) & jnp.logical_not(late))
                    def _():
                        loads[1].wait()

                layer_forward(
                    acts.at[m], mix_ref, gain_ref, up_v, down_v, keep, acts_out.at[m], last, ready,
                    lambda c: onward(m, c).start(),
                )

            @pl.when(jnp.logical_not(ahead))
            def _():
                @pl.when((m == 0) & jnp.logical_not(late))
                def _():
                    turn()

                @pl.when(last)
                def _():
                    copy_here(top_in.at[pl.ds(pl.multiple_of(m * rows, rows), rows), :], cots.at[m], tsem.at[m]).wait()

                @pl.when(jnp.logical_not(last))
                def _():
                    for j in range(per):
                        back(m, j).wait_recv()

                def send(j):
                    @pl.when(jnp.logical_not(first))
                    def _():
                        back(m, j).start()

                    @pl.when(first)
                    def _():
                        section = m * per + j
                        if j == 0:
                            @pl.when(section == 0)
                            def _():
                                keep_own.start()

                            @pl.when(section > 0)
                            def _():
                                leave(m, j, section).start()
                        else:
                            leave(m, j, section).start()

                layer_backward(
                    acts.at[m], cots.at[m], unmix_ref, gain_ref, up_tv, down_tv, keep,
                    gated, unit, pulled, spread, cots_out.at[m], send,
                )

            return carry

        lax.fori_loop(0, 2 * micro, step, 0)

        @pl.when(first)
        def _():
            keep_own.wait()
            for section in range(1, stages):
                leave(section // per, section % per, jnp.int32(section)).wait_send()

        @pl.when(jnp.logical_not(first))
        def _():
            leave(0, 0, jnp.int32(0)).wait_recv()
            entry(me).wait_send()
            for m in range(micro):
                for j in range(per):
                    back(m, j).wait_send()

        @pl.when(jnp.logical_not(last))
        def _():
            for m in range(micro):
                for c in range(chunks):
                    onward(m, c).wait_send()

        out[...] = share[...]

    vmem = pl.BlockSpec(memory_space=pltpu.VMEM)
    hbm = pl.BlockSpec(memory_space=pl.ANY)
    dma = pltpu.SemaphoreType.DMA
    block = (micro, rows, model)
    wide = (micro, chunks, rows, chunk)
    tall = embeds * rows
    return pl.pallas_call(
        body,
        in_specs=[vmem, hbm, vmem, vmem, hbm, hbm],
        out_specs=vmem,
        out_shape=jax.ShapeDtypeStruct((look, model), BF),
        scratch_shapes=[
            pltpu.VMEM(wide, BF), pltpu.VMEM(block, BF), pltpu.VMEM(wide, BF), pltpu.VMEM(block, BF),
            pltpu.VMEM((look, model), BF),
            pltpu.VMEM((model, inner), BF), pltpu.VMEM((inner, model), BF),
            pltpu.VMEM((inner, model), BF), pltpu.VMEM((model, inner), BF),
            pltpu.VMEM((micro, tall, width), F32), pltpu.VMEM((micro, rows, width), F32),
            pltpu.VMEM((micro, rows, inner), BF),
            pltpu.VMEM((tall, model), BF), pltpu.VMEM((rows, model), BF), pltpu.VMEM((rows, inner), BF),
            pltpu.VMEM((rows, model), F32), pltpu.VMEM((tall, width), BF), pltpu.VMEM((tall, model), F32),
            pltpu.VMEM((model, width), BF), pltpu.VMEM((width, model), BF), pltpu.VMEM((1, model), F32),
            dma((2,)), dma((micro,)), dma((micro, chunks)), dma((micro, chunks)),
            dma((micro, per)), dma((micro, per)),
            dma, dma((stages,)), dma((stages,)), dma, dma,
        ],
        compiler_params=pltpu.CompilerParams(
            collective_id=0, has_side_effects=True, vmem_limit_bytes=60 << 20
        ),
        name="layer_pipeline",
    )(shares, top, proj, gain, w_up, w_down)


def partner(j, tables):
    pairs = tables // 2
    order = lax.rem(j * 21, pairs * lax.axis_size("section"))
    return order // pairs, lax.rem(order, pairs)


def place(j, sign):
    sections, tables = lax.axis_size("section"), lax.axis_size("table")
    pairs = tables // 2
    step_s, step_t = partner(j, tables)
    section = lax.rem(lax.axis_index("section") + sections + sign * step_s, sections)
    pair = lax.rem(lax.axis_index("table") // 2 + pairs + sign * step_t, pairs)
    return section, pair


def greet(sections, tables):
    barrier = pltpu.get_barrier_semaphore()
    me_s, me_t = lax.axis_index("section"), lax.axis_index("table")

    def signal(d, carry):
        pl.semaphore_signal(
            barrier, inc=1,
            device_id=(lax.rem(me_s + d // tables, sections), lax.rem(me_t + lax.rem(d, tables), tables)),
            device_id_type=pl.DeviceIdType.MESH,
        )
        return carry

    lax.fori_loop(1, sections * tables, signal, 0)
    pl.semaphore_wait(barrier, sections * tables - 1)


def fetch_compress(table, wanted, counts, slots, lcb, chunk):
    sections, tables = lax.axis_size("section"), lax.axis_size("table")
    owners = sections * tables
    pairs = owners // 2
    groups = 8
    rows, width = table.shape
    samples, features = slots.shape
    cap = wanted.shape[1]
    embeds = lcb.shape[0]
    shift = cap.bit_length() - 1

    def body(idx, tab, wanted_ref, count_ref, slot_ref, lcb_ref, sent_out, mat_out, targets, shares, wide, tmp, stage, landed, mat, acc, ssem, rsem, lsem, osem):
        me_s, me_t = lax.axis_index("section"), lax.axis_index("table")
        me = me_s * tables + me_t
        wide[...] = tab[...].astype(F32)
        greet(sections, tables)

        def target(i):
            section, pair = place(i // 2, 1)
            return section, pair * 2 + lax.rem(me_t + lax.rem(i, 2), 2)

        def block(o):
            return pl.ds(pl.multiple_of(o * cap, cap), cap)

        def send(i):
            section, spot = target(i)
            return pltpu.make_async_remote_copy(
                src_ref=stage.at[block(section * tables + spot), :], dst_ref=landed.at[block(me), :],
                send_sem=ssem, recv_sem=rsem.at[i // (2 * pairs // groups)],
                device_id=(section, spot), device_id_type=pl.DeviceIdType.MESH,
            )

        own = pltpu.make_async_copy(stage.at[block(me), :], landed.at[block(me), :], lsem)

        def gather(i, carry):
            section, spot = target(i)
            base = (section * tables + spot) * cap
            for r in range(cap):
                tmp[pl.ds(r, 1), :] = wide[pl.ds(idx[base + r], 1), :]
            stage[pl.ds(pl.multiple_of(base, cap), cap), :] = tmp[...].astype(BF)

            @pl.when(i == 1)
            def _():
                own.start()

            @pl.when(i > 1)
            def _():
                send(i - 1).start()

            return carry

        lax.fori_loop(0, owners, gather, 0)
        send(owners - 1).start()
        keep = pltpu.make_async_copy(stage, sent_out, osem.at[0])
        keep.start()

        tiled = jnp.concatenate([lcb_ref[...].astype(F32)] * 2, axis=0).astype(BF)
        zero = jnp.zeros((), BF)
        lane = lax.broadcasted_iota(jnp.int32, (2 * cap, features), 0)
        row = (lax.broadcasted_iota(jnp.int32, (16, features), 0) // embeds).astype(F32).astype(BF)

        def select(p, carry):
            parts = []
            for h in range(2):
                slot = slot_ref[pl.ds(p * 2 + h, 1), :]
                pair = lax.shift_right_logical(slot, shift + 1)
                spot = slot & (2 * cap - 1)
                picks = jnp.where(lane == spot, 1.0, 0.0).astype(BF)
                pair16 = jnp.broadcast_to(pair.astype(F32), (16, features)).astype(BF)
                spread = jnp.concatenate(
                    [jnp.where(pair16 == row + jnp.asarray(float(o), BF), tiled, zero) for o in range(0, pairs, 2)],
                    axis=0,
                )
                got = lax.dot_general(spread, picks, NT, preferred_element_type=F32)
                parts.append(got.reshape(pairs, embeds, 2 * cap))
            mat[:, pl.ds(pl.multiple_of(p * 2 * embeds, 2 * embeds), 2 * embeds), :] = jnp.concatenate(parts, axis=1).astype(BF)
            return carry

        lax.fori_loop(0, samples // 2, select, 0)
        save = pltpu.make_async_copy(mat, mat_out, osem.at[1])
        save.start()
        live = jnp.broadcast_to(count_ref[...].astype(F32), (owners, owners)).T
        spot = lax.broadcasted_iota(jnp.int32, (owners, cap), 1).astype(F32)
        targets[...] = jnp.where(spot < live[:, :cap], wanted_ref[...], rows)
        acc[...] = jnp.zeros_like(acc)
        own.wait()

        def collect(g, carry):
            span = 2 * cap * (pairs // groups)

            @pl.when(g == 0)
            def _():
                part = pl.ds(0, span - cap)
                pltpu.make_async_copy(stage.at[part, :], landed.at[part, :], rsem.at[g]).wait()

            @pl.when(g > 0)
            def _():
                part = pl.ds(0, span)
                pltpu.make_async_copy(stage.at[part, :], landed.at[part, :], rsem.at[g]).wait()

            total = acc[...]
            for e in range(pairs // groups):
                section, pair = place(g * (pairs // groups) + e, -1)
                o = section * (tables // 2) + pair
                total += jnp.dot(
                    mat[o], landed[pl.ds(pl.multiple_of(o * 2 * cap, 2 * cap), 2 * cap), :],
                    preferred_element_type=F32,
                )
            acc[...] = total
            return carry

        lax.fori_loop(0, groups, collect, 0)
        for k in range(embeds):
            at = (k * width) % chunk
            shares[k * width // chunk, :, at : at + width] = acc[pl.ds(k, samples, stride=embeds), :].astype(BF)
        part = pl.ds(0, (owners - 1) * cap)
        pltpu.make_async_copy(stage.at[part, :], landed.at[part, :], ssem).wait()
        keep.wait()
        save.wait()

    vmem = pl.BlockSpec(memory_space=pltpu.VMEM)
    hbm = pl.BlockSpec(memory_space=pl.ANY)
    dma = pltpu.SemaphoreType.DMA
    return pl.pallas_call(
        body,
        in_specs=[pl.BlockSpec(memory_space=pltpu.SMEM), vmem, vmem, vmem, vmem, vmem],
        out_specs=[hbm, hbm, vmem, vmem],
        out_shape=[
            jax.ShapeDtypeStruct((owners * cap, width), BF),
            jax.ShapeDtypeStruct((pairs, samples * embeds, 2 * cap), BF),
            jax.ShapeDtypeStruct((owners, cap), jnp.int32),
            jax.ShapeDtypeStruct((embeds * width // chunk, samples, chunk), BF),
        ],
        scratch_shapes=[
            pltpu.VMEM((rows, width), F32), pltpu.VMEM((cap, width), F32),
            pltpu.VMEM((owners * cap, width), BF), pltpu.VMEM((owners * cap, width), BF),
            pltpu.VMEM((pairs, samples * embeds, 2 * cap), BF), pltpu.VMEM((samples * embeds, width), F32),
            dma, dma((groups,)), dma, dma((2,)),
        ],
        compiler_params=pltpu.CompilerParams(collective_id=1, has_side_effects=True, vmem_limit_bytes=60 << 20),
        name="fetch_compress",
    )(wanted.reshape(-1), table, wanted, counts, slots, lcb)


def expand_return(matrix, grads, cap):
    sections, tables = lax.axis_size("section"), lax.axis_size("table")
    owners = sections * tables
    pairs, outs, slots = matrix.shape
    samples, model = grads.shape
    embeds = outs // samples
    width = model // embeds
    groups = 8
    per = pairs // groups

    def body(mat_in, grad, landed, done, mat, wide, tall, stage, msem, ssem, rsem, lsem):
        me_s, me_t = lax.axis_index("section"), lax.axis_index("table")
        me = me_s * tables + me_t

        def load(j):
            section, pair = place(j, 1)
            o = section * (tables // 2) + pair
            return pltpu.make_async_copy(mat_in.at[o], mat.at[j], msem.at[j])

        def begin(j, carry):
            load(j).start()
            return carry

        lax.fori_loop(0, pairs, begin, 0)
        for k in range(embeds):
            wide[pl.ds(k, samples, stride=embeds), :] = grad[:, k * width : (k + 1) * width].astype(F32)
        tall[...] = wide[...].astype(BF)
        greet(sections, tables)

        def block(o):
            return pl.ds(pl.multiple_of(o * cap, cap), cap)

        def send(section, spot):
            return pltpu.make_async_remote_copy(
                src_ref=stage.at[block(section * tables + spot), :], dst_ref=landed.at[block(me), :],
                send_sem=ssem, recv_sem=rsem, device_id=(section, spot), device_id_type=pl.DeviceIdType.MESH,
            )

        own = pltpu.make_async_copy(stage.at[block(me), :], landed.at[block(me), :], lsem)

        def pair_out(j):
            section, pair = place(j, 1)

            @pl.when(j == 0)
            def _():
                own.start()
                send(me_s, me_t + 1 - 2 * lax.rem(me_t, 2)).start()

            @pl.when(j > 0)
            def _():
                for b in range(2):
                    send(section, pair * 2 + b).start()

        def work(j, carry):
            section, pair = place(j, 1)
            o = section * (tables // 2) + pair
            load(j).wait()
            got = lax.dot_general(mat[j], tall[...], TN, preferred_element_type=F32)
            stage[pl.ds(pl.multiple_of(o * slots, slots), slots), :] = got.astype(BF)

            @pl.when(j > 0)
            def _():
                pair_out(j - 1)

            return carry

        lax.fori_loop(0, pairs, work, 0)
        pair_out(jnp.int32(pairs - 1))
        own.wait()
        part = pl.ds(0, (owners - 1) * cap)
        pltpu.make_async_copy(stage.at[part, :], landed.at[part, :], rsem).wait()
        pltpu.make_async_copy(stage.at[part, :], landed.at[part, :], ssem).wait()
        done[...] = jnp.zeros_like(done)

    vmem = pl.BlockSpec(memory_space=pltpu.VMEM)
    hbm = pl.BlockSpec(memory_space=pl.ANY)
    dma = pltpu.SemaphoreType.DMA
    return pl.pallas_call(
        body,
        in_specs=[hbm, vmem],
        out_specs=[hbm, vmem],
        out_shape=[
            jax.ShapeDtypeStruct((owners * cap, width), BF),
            jax.ShapeDtypeStruct((8, 128), F32),
        ],
        scratch_shapes=[
            pltpu.VMEM(matrix.shape, BF), pltpu.VMEM((outs, width), F32), pltpu.VMEM((outs, width), BF),
            pltpu.VMEM((owners * cap, width), BF), dma((pairs,)), dma, dma, dma,
        ],
        compiler_params=pltpu.CompilerParams(collective_id=2, has_side_effects=True, vmem_limit_bytes=60 << 20),
        name="expand_return",
    )(matrix, grads)[0]


def per_device(
    emb_table,
    lcb_weight,
    fm_proj,
    norm_gain,
    w_up,
    w_down,
    top_grad,
    lookup_slot,
    wanted_rows,
    row_counts,
):
    section_count = lax.axis_size("section")
    cap = wanted_rows.shape[2]

    model_width = top_grad.shape[3]
    sent, matrix, targets, shares = fetch_compress(
        emb_table, wanted_rows[0], row_counts, lookup_slot[0], lcb_weight, CHUNK
    )
    lead_share = layer_pipeline(
        shares,
        top_grad.reshape(-1, model_width),
        fm_proj[0],
        norm_gain,
        w_up[0],
        w_down[0],
        section_count,
        MICRO_ROWS,
    )
    returned = expand_return(matrix, lead_share, cap)
    return scatter_rows(returned, sent, targets.reshape(-1), emb_table.shape[0], DECAY_WEIGHT)


def solution(mesh):
    in_specs = (
        P(("section", "table"), None),
        P(),
        P("section", None, None),
        P("section", None),
        P("section", None, None),
        P("section", None, None),
        P("table", None, None, None),
        P("table", "section", None),
        P(("section", "table"), None, None),
        P(("section", "table"), None),
    )
    out_specs = P(("section", "table"), None)
    return jax.shard_map(
        per_device, mesh=mesh, in_specs=in_specs, out_specs=out_specs, check_vma=False
    )
```
